512 devices in a mesh: req: 16 (over x, y_lo, core), blk: 32 (over z, y_hi).
Axes of the slice: x: 4, y: 4 (y_hi: 2, y_lo: 2; y = y_hi * 2 + y_lo), z: 16, core: 2. Of those that a mesh axis runs over, the one named last changes fastest.
Arguments:
- queries: bfloat16 [16, 32, 512, 512], P('req', 'blk'), may hold values from -6 to 6
- keys: bfloat16 [16, 32, 512, 256], P('req', 'blk'), may hold values from -25 to 25
- values: bfloat16 [16, 32, 512, 256], P('req', 'blk'), may hold values from -6 to 6
- block_map: int32 [16, 8, 2], P('req'), may hold values from 0 to 15, as said below
- lengths: int32 [16], P('req'), may hold values from 1024 to 4096
- group_of_prompt: int32 [16], replicated, may hold values from 0 to 15, each once
- decode_rank: int32 [16, 32], P('req'), may hold values from 0 to 31, as said below
Outputs:
- attended: bfloat16 [16, 32, 512, 512], P('req', 'blk')
- cache: bfloat16 [16, 4096, 2048], P('req', 'blk')
The draws below stay inside these ranges and needn't reach their ends.
Inputs may be any that keep to these rules, and one draw needn't show every extreme that they name: In each group, block_map[g] holds each of 0 to 15 once, and the two halves of each slot hold blocks b and 15 - b, in either order. `decode_rank`: each group's row holds each of 0 to 31 once.
All inputs are finite; a program needn't handle non-finite values.
Results may differ from the reference program's by a relative error of at most 0.0098.
Values may be sent and summed in bfloat16 or wider, within the bound.
A program may use at most 64 MiB of HBM per device.

```python
import math
import jax
import jax.numpy as jnp
from jax import lax

QUERY_HEADS = 16
KEY_VALUE_HEADS = 8
HEAD_SIZE = 128
HEAD_DIVISIONS = 4
TOK_DEV = 512
BLOCK = 256
Q_DEV = 4
KV_DEV = 2
SLOTS = 8
PROMPT_CAPACITY = 4096
DEC_DEV = 128
N_REQ = 16
N_BLK = 32


def draw_keys(key, part):
    scale_key, noise_key = jax.random.split(jax.random.fold_in(key, 7), 2)
    spread = jnp.exp(jax.random.uniform(scale_key, (N_REQ, N_BLK, TOK_DEV, KV_DEV, 1), jnp.float32, math.log(2.7), math.log(3.3)))
    noise_part = jnp.clip(jax.random.normal(noise_key, (N_REQ, N_BLK, TOK_DEV, KV_DEV, HEAD_SIZE), jnp.float32), -5.0, 5.0)
    return (noise_part * spread).reshape(N_REQ, N_BLK, TOK_DEV, KV_DEV * HEAD_SIZE).astype(jnp.bfloat16)


def draw_block_map(key, part):
    order_key, flip_key = jax.random.split(jax.random.fold_in(key, 11), 2)
    key_list = jax.random.split(order_key, N_REQ)
    ordering = jax.vmap(lambda subkey: jax.random.permutation(subkey, SLOTS))(key_list).astype(jnp.int32)
    mirrored = (2 * SLOTS - 1 - ordering).astype(jnp.int32)
    flipped = jax.random.randint(flip_key, (N_REQ, SLOTS), 0, 2, jnp.int32)
    first_half = jnp.where(flipped == 1, mirrored, ordering)
    second_half = jnp.where(flipped == 1, ordering, mirrored)
    return jnp.stack([first_half, second_half], axis=2).astype(jnp.int32)


def draw_decode_rank(key, part):
    key_list = jax.random.split(jax.random.fold_in(key, 13), N_REQ)
    ordering = jax.vmap(lambda subkey: jax.random.permutation(subkey, N_BLK))(key_list)
    return ordering.astype(jnp.int32)


def set_ends(drawn, stream_key, least, top_value):
    longest = drawn.shape.index(max(drawn.shape))
    spots = []
    for shift in (0, 1):
        where = [jax.random.randint(jax.random.fold_in(stream_key, axis), (), 0, length) for axis, length in enumerate(drawn.shape)]
        where[longest] = (where[longest] + shift) % drawn.shape[longest]
        spots.append(tuple(where))
    return drawn.at[spots[0]].set(least).at[spots[1]].set(top_value)


def levels(rng, shape, cuts, low, largest):
    loudness = 1.0
    for dim, shards_of in cuts:
        draws = jax.random.uniform(jax.random.fold_in(jax.random.fold_in(rng, 6), dim), (shards_of,), jnp.float32, low / len(cuts), largest / len(cuts))
        loudness = loudness * jnp.repeat(jnp.exp(draws), shape[dim] // shards_of).reshape((-1,) + (1,) * (len(shape) - 1 - dim))
    return loudness


def centred(own_key, shape, scale, reach, cuts=(), kind=jnp.bfloat16):
    values = jax.random.normal(own_key, shape, jnp.float32) * scale
    if len(cuts) > 0:
        values = levels(own_key, shape, cuts, -0.22, 0.18) * values
    return jnp.clip(values, min=-reach, max=reach).astype(kind)


def setup_inputs(seed: int = 0) -> dict:
    seeds = jax.random.split(jax.random.key(seed), 8)
    queries = centred(seeds[0], (N_REQ, N_BLK, TOK_DEV, Q_DEV * HEAD_SIZE), 1.0, 6.0, ((0, 16), (1, 32)))
    keys = draw_keys(jax.random.fold_in(seeds[7], 71), 0)
    values = centred(seeds[2], (N_REQ, N_BLK, TOK_DEV, KV_DEV * HEAD_SIZE), 1.0, 6.0, ((0, 16), (1, 32)))
    block_map = draw_block_map(jax.random.fold_in(seeds[7], 71), 0)
    lengths = set_ends(jax.random.randint(seeds[4], (N_REQ,), PROMPT_CAPACITY // 4, PROMPT_CAPACITY + 1), jax.random.fold_in(seeds[4], 1), PROMPT_CAPACITY // 4, PROMPT_CAPACITY).astype(jnp.int32)
    group_of_prompt = jax.random.permutation(seeds[5], N_REQ).astype(jnp.int32)
    decode_rank = draw_decode_rank(jax.random.fold_in(seeds[7], 71), 0)
    return dict(queries=queries, keys=keys, values=values, block_map=block_map, lengths=lengths, group_of_prompt=group_of_prompt, decode_rank=decode_rank)


cap_value = 50.0
query_scale = 1.0 / 12.0
rope_base = 10000.0


def apply_rotary(row_block, token_position, head_count):
    row_count = row_block.shape[0]
    head_width = row_block.shape[1] // head_count
    half_width = head_width // 2
    shaped = row_block.astype(jnp.float32).reshape(row_count, head_count, head_width)
    frequency = jnp.exp(-math.log(rope_base) * (2.0 * jnp.arange(half_width, dtype=jnp.float32)) / head_width)
    angles = token_position.astype(jnp.float32)[:, None] * frequency[None, :]
    cosine = jnp.cos(angles)[:, None, :]
    sine_part = jnp.sin(angles)[:, None, :]
    front_half = shaped[:, :, :half_width]
    second = shaped[:, :, half_width:]
    turned = jnp.concatenate([front_half * cosine - second * sine_part, second * cosine + front_half * sine_part], axis=2)
    return turned.reshape(row_count, head_count * head_width)


def whole_rows(array, cache_slot_count):
    width = array.shape[2]
    shaped = array.reshape(cache_slot_count, HEAD_DIVISIONS, TOK_DEV, width)
    return jnp.transpose(shaped, (0, 2, 1, 3)).reshape(PROMPT_CAPACITY, HEAD_DIVISIONS * width)


def reference(queries, keys, values, block_map, lengths, group_of_prompt, decode_rank):
    cache_slot_count = N_BLK // HEAD_DIVISIONS
    key_value_width = KEY_VALUE_HEADS * HEAD_SIZE
    group_portion = QUERY_HEADS // KEY_VALUE_HEADS
    row_ids = jnp.arange(PROMPT_CAPACITY, dtype=jnp.int32)
    query_extent = 512 if PROMPT_CAPACITY % 512 == 0 else PROMPT_CAPACITY
    group_ids = jnp.arange(N_REQ, dtype=jnp.int32)

    def one_group(element):
        query_dev, key_dev, value_dev, block_table, rank_of, group_id = element
        query_rows = whole_rows(query_dev, cache_slot_count)
        key_row_list = whole_rows(key_dev, cache_slot_count)
        value_row_list = whole_rows(value_dev, cache_slot_count)
        length = jnp.sum(jnp.where(group_of_prompt == group_id, lengths, 0))
        flat_map = block_table.reshape(-1)
        token_position = (flat_map[row_ids // BLOCK] * BLOCK + row_ids % BLOCK).astype(jnp.int32)
        query_rot = (apply_rotary(query_rows, token_position, QUERY_HEADS) * query_scale).astype(jnp.bfloat16)
        rotated_key = apply_rotary(key_row_list, token_position, KEY_VALUE_HEADS).astype(jnp.bfloat16)
        widened_keys = rotated_key.astype(jnp.float32).reshape(PROMPT_CAPACITY, KEY_VALUE_HEADS, HEAD_SIZE)
        widened_values = value_row_list.astype(jnp.float32).reshape(PROMPT_CAPACITY, KEY_VALUE_HEADS, HEAD_SIZE)

        def one_block(pair):
            query_piece, query_pos = pair
            query_head_rows = query_piece.astype(jnp.float32).reshape(query_extent, KEY_VALUE_HEADS, group_portion, HEAD_SIZE)
            scores = jnp.einsum("qkgd,nkd->kgqn", query_head_rows, widened_keys, precision=lax.Precision.HIGHEST)
            capped = cap_value * jnp.tanh(scores / cap_value)
            allowed = token_position[None, :] <= query_pos[:, None]
            expo_vals = jnp.where(allowed[None, None], jnp.exp(capped), jnp.float32(0.0))
            weight = lax.optimization_barrier(expo_vals.astype(jnp.bfloat16)).astype(jnp.float32)
            numerator = jnp.einsum("kgqn,nkd->qkgd", weight, widened_values, precision=lax.Precision.HIGHEST)
            denominator = jnp.sum(expo_vals, axis=3)
            output = numerator / jnp.transpose(denominator, (2, 0, 1))[..., None]
            output = output.reshape(query_extent, QUERY_HEADS * HEAD_SIZE)
            return jnp.where((query_pos < length)[:, None], output, jnp.float32(0.0)).astype(jnp.bfloat16)

        attended = lax.map(one_block, (query_rot.reshape(PROMPT_CAPACITY // query_extent, query_extent, QUERY_HEADS * HEAD_SIZE), token_position.reshape(PROMPT_CAPACITY // query_extent, query_extent)))
        attended = attended.reshape(cache_slot_count, TOK_DEV, HEAD_DIVISIONS, Q_DEV * HEAD_SIZE)
        attended = jnp.transpose(attended, (0, 2, 1, 3)).reshape(N_BLK, TOK_DEV, Q_DEV * HEAD_SIZE)
        joined = jnp.concatenate([rotated_key, value_row_list], axis=1)
        joined = jnp.where((token_position < length)[:, None], joined, jnp.zeros_like(joined))
        target = (rank_of[token_position % N_BLK] * DEC_DEV + token_position // N_BLK).astype(jnp.int32)
        cache_rows = jnp.zeros((PROMPT_CAPACITY, 2 * key_value_width), jnp.bfloat16).at[target].set(joined)
        return attended, cache_rows

    attended, cache_rows = lax.map(one_group, (queries, keys, values, block_map, decode_rank, group_ids))
    return attended, cache_rows
```

```python
import functools
import math

import jax
import jax.numpy as jnp
from jax import lax
from jax.experimental import pallas as pl
from jax.experimental.pallas import tpu as pltpu
from jax.sharding import PartitionSpec as P

SLOTS = 8
HEAD_DIVISIONS = 4
KV_DEV = 2
HEAD = 128
HALF_TURN = 64
BLOCK = 256
RESIDUES = 32
CAP = 50.0
QUERY_SCALE = 1.0 / 12.0
ROPE_BASE = 10000.0
ORDER = (0, 1, 7, 2, 6, 3, 5, 4)
MESH = pl.DeviceIdType.MESH


def pick(condition, value):
    return jnp.where(condition, value, 0)


def kernel(
    q_hbm, k_hbm, v_hbm, table, length_ref, group_of, rank_of,
    out_ref, cache_ref,
    q_raw, kbuf, vbuf, qrot, krot, num, den, cos_row, sin_row, cos_blk, sin_blk,
    choose, chosen, arrived, lens,
    load_sem, send_sem, recv_sem, pick_send, pick_recv, len_send, len_recv,
):
    req = lax.axis_index("req")
    me = lax.axis_index("blk")
    slot = me // HEAD_DIVISIONS
    head_group = me % HEAD_DIVISIONS
    ring = SLOTS * HEAD_DIVISIONS
    right = (me + HEAD_DIVISIONS) % ring
    left = (me + ring - HEAD_DIVISIONS) % ring

    def quad_peer(e):
        low = head_group % 2
        high = head_group // 2
        if e & 1:
            low = 1 - low
        if e & 2:
            high = 1 - high
        return high * 2 + low

    core = req % 2
    y_low = (req // 2) % 2
    x = req // 4
    mate = req + 1 - 2 * core
    y_mate = req + 2 - 4 * y_low
    x_mates = [((x + i) % 4) * 4 + req % 4 for i in (1, 2, 3)]

    loads = [
        pltpu.make_async_copy(q_hbm, q_raw, load_sem.at[0]),
        pltpu.make_async_copy(k_hbm, kbuf.at[0], load_sem.at[1]),
        pltpu.make_async_copy(v_hbm, vbuf.at[0], load_sem.at[2]),
    ]
    for load in loads:
        load.start()

    barrier = pltpu.get_barrier_semaphore()
    partners = [(req, right), (req, left)]
    partners += [(req, slot * HEAD_DIVISIONS + quad_peer(e)) for e in (1, 2, 3)]
    partners += [(mate, me), (y_mate, me)] + [(xm, me) for xm in x_mates]
    for partner in partners:
        pl.semaphore_signal(barrier, inc=1, device_id=partner, device_id_type=MESH)
    pl.semaphore_wait(barrier, len(partners))

    def hop(side, turn, chunk):
        half = chunk // 2
        rows = pl.ds(half * BLOCK, BLOCK)
        is_value = chunk % 2 == 1
        buf = vbuf if is_value else kbuf
        if side == 0:
            source, target, device = turn, turn + 1, right
        else:
            source, target, device = (SLOTS - turn) % SLOTS, SLOTS - turn - 1, left
        if turn == 0:
            src = (v_hbm if is_value else k_hbm).at[rows]
        else:
            src = buf.at[source, rows]
        return pltpu.make_async_remote_copy(
            src_ref=src,
            dst_ref=buf.at[target, rows],
            send_sem=send_sem.at[side, turn, chunk],
            recv_sem=recv_sem.at[target, chunk],
            device_id=(req, device),
            device_id_type=MESH,
        )

    def travels(side, turn, chunk):
        if turn < 3:
            return True
        return turn == 3 and (chunk // 2 == side)

    sent = []
    for chunk in range(4):
        for side in range(2):
            copy = hop(side, 0, chunk)
            copy.start()
            sent.append(copy)

    lens[req] = jnp.full((8, 128), length_ref[0], jnp.int32)

    def len_copy(index, start, size, to):
        rows = lens.at[pl.ds(start, size)]
        return pltpu.make_async_remote_copy(
            src_ref=rows, dst_ref=rows, send_sem=len_send.at[index], recv_sem=len_recv.at[index],
            device_id=(to, me), device_id_type=MESH,
        )

    lane = lax.broadcasted_iota(jnp.int32, (BLOCK, HEAD), 1)
    row = lax.broadcasted_iota(jnp.int32, (BLOCK, HEAD), 0)
    pair = jnp.where(lane < HALF_TURN, lane, lane - HALF_TURN).astype(jnp.float32)
    frequency = jnp.exp(-math.log(ROPE_BASE) * (2.0 * pair) / HEAD)
    sign = jnp.where(lane < HALF_TURN, -1.0, 1.0)
    angle = row.astype(jnp.float32) * frequency
    cos_row[...] = jnp.cos(angle)
    sin_row[...] = jnp.sin(angle) * sign

    blk_row = lax.broadcasted_iota(jnp.int32, (2 * SLOTS, HEAD), 0)
    blk_of = jnp.zeros((2 * SLOTS, HEAD), jnp.int32)
    for s in range(SLOTS):
        for half in range(2):
            blk_of = jnp.where(blk_row == 2 * s + half, table[0, s, half], blk_of)
    base = (blk_of * BLOCK).astype(jnp.float32) * frequency[: 2 * SLOTS]
    cos_blk[...] = jnp.cos(base)
    sin_blk[...] = jnp.sin(base) * sign[: 2 * SLOTS]

    def turn_tables(source, half):
        at = pl.ds(2 * source + half, 1)
        cos_b = jnp.broadcast_to(cos_blk[at, :], (BLOCK, HEAD))
        sin_b = jnp.broadcast_to(sin_blk[at, :], (BLOCK, HEAD))
        cos_r, sin_r = cos_row[...], sin_row[...]
        return cos_b * cos_r - sin_b * sin_r, sin_b * cos_r + cos_b * sin_r

    def rotated(part, cosine, sine):
        part = part.astype(jnp.float32)
        return part * cosine + pltpu.roll(part, HALF_TURN, 1) * sine

    residue = []
    for h in range(HEAD_DIVISIONS):
        wanted = slot * HEAD_DIVISIONS + h
        found = jnp.int32(0)
        for r in range(RESIDUES):
            found = found + pick(rank_of[0, r] == wanted, r)
        residue.append(found)
    c_row = lax.broadcasted_iota(jnp.int32, (64, 2 * BLOCK), 0)
    c_col = lax.broadcasted_iota(jnp.int32, (64, 2 * BLOCK), 1)
    wanted_col = ((c_row % 16) // 8) * BLOCK + (c_row % 8) * RESIDUES
    for h in range(HEAD_DIVISIONS):
        wanted_col = wanted_col + pick(c_row // 16 == h, residue[h])
    choose[...] = jnp.where(c_col == wanted_col, 1.0, 0.0).astype(jnp.bfloat16)

    mate_copy = len_copy(0, req, 1, mate)
    mate_copy.start()
    sent.append(mate_copy)

    for load in loads:
        load.wait()

    for half in range(2):
        cosine, sine = turn_tables(slot, half)
        for head in range(2 * KV_DEV):
            part = q_raw[half * BLOCK : (half + 1) * BLOCK, head * HEAD : (head + 1) * HEAD]
            turned = rotated(part, cosine, sine) * QUERY_SCALE
            qrot[head // 2, (head % 2) * 2 + half] = turned.astype(jnp.bfloat16)
    num[...] = jnp.zeros_like(num)
    den[...] = jnp.zeros_like(den)

    q_block = [table[0, slot, half] for half in range(2)]
    tile_row = lax.broadcasted_iota(jnp.int32, (BLOCK, BLOCK), 0)
    tile_col = lax.broadcasted_iota(jnp.int32, (BLOCK, BLOCK), 1)

    def prepare(order):
        j = ORDER[order]
        source = (slot + SLOTS - j) % SLOTS
        for half in range(2):
            cosine, sine = turn_tables(source, half)
            for head in range(KV_DEV):
                part = kbuf[j, half * BLOCK : (half + 1) * BLOCK, head * HEAD : (head + 1) * HEAD]
                krot[head, half * BLOCK : (half + 1) * BLOCK, :] = rotated(part, cosine, sine).astype(
                    jnp.bfloat16
                )
        for head in range(KV_DEV):
            for kind in range(2):
                cols = slice(head * HEAD, (head + 1) * HEAD)
                data = krot[head] if kind == 0 else vbuf[j, :, cols]
                rows = jnp.dot(choose[...], data, preferred_element_type=jnp.float32)
                rows = rows.astype(jnp.bfloat16)
                first = kind * KV_DEV * HEAD + head * HEAD
                for h in range(HEAD_DIVISIONS):
                    chosen[h, order, :, first : first + HEAD] = rows[h * 16 : (h + 1) * 16]

    def attend(order, head):
        j = ORDER[order]
        source = (slot + SLOTS - j) % SLOTS
        for half in range(2):
            k_block = table[0, source, half]

            def tile(t, carry):
                k_part = krot[head, half * BLOCK : (half + 1) * BLOCK, :]
                v_part = vbuf[j, half * BLOCK : (half + 1) * BLOCK, head * HEAD : (head + 1) * HEAD]
                q_block_now = jnp.where(t % 2 == 0, q_block[0], q_block[1])
                scores = lax.dot_general(
                    qrot[head, t], k_part, (((1,), (1,)), ((), ())),
                    preferred_element_type=jnp.float32,
                )
                expo = jnp.exp(CAP * jnp.tanh(scores * (1.0 / CAP)))
                behind = (q_block_now - k_block) * BLOCK
                expo = jnp.where(tile_col - tile_row <= behind, expo, 0.0)
                den[head, t] += expo[:, :HEAD] + expo[:, HEAD:]
                num[head, t] += jnp.dot(
                    expo.astype(jnp.bfloat16), v_part, preferred_element_type=jnp.float32
                )
                return carry

            lax.fori_loop(0, 4, tile, 0)

    def share(batch, first, count):
        for e in (1, 2, 3):
            peer = quad_peer(e)
            copy = pltpu.make_async_remote_copy(
                src_ref=chosen.at[peer, pl.ds(first, count)],
                dst_ref=arrived.at[e, pl.ds(first, count)],
                send_sem=pick_send.at[e, batch],
                recv_sem=pick_recv.at[e, batch],
                device_id=(req, slot * HEAD_DIVISIONS + peer),
                device_id_type=MESH,
            )
            copy.start()
            sent.append(copy)
            shares.append(copy)

    shares = []

    prepare(0)
    for head in range(KV_DEV):
        attend(0, head)

    len_waits = [mate_copy]
    for turn in range(1, 5):
        for chunk in range(4):
            for side in range(2):
                if turn == 4 and chunk // 2 != side:
                    continue
                hop(side, turn - 1, chunk).wait_recv()
                if travels(side, turn, chunk):
                    copy = hop(side, turn, chunk)
                    copy.start()
                    sent.append(copy)
        if turn == 1:
            mate_copy.wait_recv()
            y_copy = len_copy(1, (req // 2) * 2, 2, y_mate)
            y_copy.start()
            sent.append(y_copy)
        if turn == 2:
            y_copy.wait_recv()
            x_copies = [len_copy(2 + i, (req // 4) * 4, 4, x_mates[i]) for i in range(3)]
            for copy in x_copies:
                copy.start()
                sent.append(copy)
        if turn == 3:
            share(0, 0, 5)
        if turn < 4:
            for order in (2 * turn - 1, 2 * turn):
                prepare(order)
                for head in range(KV_DEV):
                    attend(order, head)
        else:
            share(1, 5, 2)
            prepare(7)
            attend(7, 0)
            share(2, 7, 1)
            attend(7, 1)

    for copy in x_copies:
        copy.wait_recv()
    length = jnp.zeros((8, 128), jnp.int32)
    for p in range(16):
        length = length + pick(group_of[p] == req, lens[p])
    length = length[0:1, :]

    for half in range(2):
        rows = slice(half * BLOCK, (half + 1) * BLOCK)
        live = row + q_block[half] * BLOCK < jnp.broadcast_to(length, (BLOCK, HEAD))
        for head in range(2 * KV_DEV):
            total = jnp.sum(den[head // 2, (head % 2) * 2 + half], axis=1, keepdims=True)
            value = num[head // 2, (head % 2) * 2 + half] / total
            out_ref[rows, head * HEAD : (head + 1) * HEAD] = jnp.where(live, value, 0.0).astype(jnp.bfloat16)

    own_residue = jnp.int32(0)
    for r in range(RESIDUES):
        own_residue = own_residue + pick(rank_of[0, r] == me, r)
    p_row = lax.broadcasted_iota(jnp.int32, (HEAD, HEAD), 0)
    p_col = lax.broadcasted_iota(jnp.int32, (HEAD, HEAD), 1)
    place = p_col % 8
    for order in range(8):
        source = (slot + SLOTS - ORDER[order]) % SLOTS
        for half in range(2):
            place = place + pick(p_col // 8 == 2 * order + half, table[0, source, half] * 8)
    kept = p_row * RESIDUES + own_residue < jnp.broadcast_to(length, (HEAD, HEAD))
    placed = jnp.where(jnp.logical_and(place == p_row, kept), 1.0, 0.0).astype(jnp.bfloat16)

    for copy in shares:
        copy.wait_recv()
    width = KV_DEV * HEAD
    for e in range(4):
        from_head = head_group if e == 0 else quad_peer(e)
        data = chosen[head_group] if e == 0 else arrived[e]
        data = data.reshape(8 * 16, 2 * width)
        moved = jnp.dot(placed, data, preferred_element_type=jnp.float32).astype(jnp.bfloat16)
        for kind in range(2):
            start = pl.multiple_of(kind * HEAD_DIVISIONS * width + from_head * width, width)
            cache_ref[:, pl.ds(start, width)] = moved[:, kind * width : (kind + 1) * width]

    for copy in sent:
        copy.wait_send()


def on_device(queries, keys, values, block_map, lengths, group_of_prompt, decode_rank):
    rows = queries.shape[2]
    wide, narrow = queries.shape[3], keys.shape[3]
    anywhere = pl.BlockSpec(memory_space=pl.ANY)
    scalars = pl.BlockSpec(memory_space=pltpu.SMEM)
    vmem = pl.BlockSpec(memory_space=pltpu.VMEM)
    dma = pltpu.SemaphoreType.DMA
    bf16, f32 = jnp.bfloat16, jnp.float32
    out, cache = pl.pallas_call(
        kernel,
        out_shape=(
            jax.ShapeDtypeStruct((rows, wide), bf16),
            jax.ShapeDtypeStruct((rows // HEAD_DIVISIONS, 2048), bf16),
        ),
        in_specs=[anywhere] * 3 + [scalars] * 4,
        out_specs=(vmem, vmem),
        scratch_shapes=[
            pltpu.VMEM((rows, wide), bf16),
            pltpu.VMEM((SLOTS, rows, narrow), bf16),
            pltpu.VMEM((SLOTS, rows, narrow), bf16),
            pltpu.VMEM((KV_DEV, 4, BLOCK, HEAD), bf16),
            pltpu.VMEM((KV_DEV, rows, HEAD), bf16),
            pltpu.VMEM((KV_DEV, 4, BLOCK, HEAD), f32),
            pltpu.VMEM((KV_DEV, 4, BLOCK, HEAD), f32),
            pltpu.VMEM((BLOCK, HEAD), f32),
            pltpu.VMEM((BLOCK, HEAD), f32),
            pltpu.VMEM((2 * SLOTS, HEAD), f32),
            pltpu.VMEM((2 * SLOTS, HEAD), f32),
            pltpu.VMEM((64, 2 * BLOCK), bf16),
            pltpu.VMEM((HEAD_DIVISIONS, SLOTS, 16, 2 * narrow), bf16),
            pltpu.VMEM((HEAD_DIVISIONS, SLOTS, 16, 2 * narrow), bf16),
            pltpu.VMEM((16, 8, 128), jnp.int32),
            dma((3,)),
            dma((2, 4, 4)),
            dma((SLOTS, 4)),
            dma((4, 3)),
            dma((4, 3)),
            dma((5,)),
            dma((5,)),
        ],
        compiler_params=pltpu.CompilerParams(collective_id=0, has_side_effects=True),
    )(
        queries.reshape(rows, wide), keys.reshape(rows, narrow), values.reshape(rows, narrow),
        block_map, lengths, group_of_prompt, decode_rank,
    )
    return out[None, None], cache[None]


def solution(mesh):
    placed = (
        P("req", "blk", None, None),
        P("req", "blk", None, None),
        P("req", "blk", None, None),
        P("req", None, None),
        P("req"),
        P(),
        P("req", None),
    )
    return jax.shard_map(
        on_device,
        mesh=mesh,
        in_specs=placed,
        out_specs=(P("req", "blk", None, None), P("req", "blk", None)),
        check_vma=False,
    )
```

```python
import functools
import math

import jax
import jax.numpy as jnp
from jax import lax
from jax.experimental import pallas as pl
from jax.experimental.pallas import tpu as pltpu
from jax.sharding import PartitionSpec as P

SLOTS = 8
HEAD_DIVISIONS = 4
KV_DEV = 2
HEAD = 128
HALF_TURN = 64
BLOCK = 256
RESIDUES = 32
CAP = 50.0
QUERY_SCALE = 1.0 / 12.0
ROPE_BASE = 10000.0
ORDER = (0, 1, 7, 2, 6, 3, 5, 4)
MESH = pl.DeviceIdType.MESH


def pick(condition, value):
    return jnp.where(condition, value, 0)


def kernel(
    q_hbm, k_hbm, v_hbm, table, length_ref, group_of, rank_of,
    out_ref, cache_ref,
    q_raw, kbuf, vbuf, qrot, krot, num, den, cos_row, sin_row, cos_blk, sin_blk,
    choose, chosen, arrived, lens, kpair, vpair, kept_weight,
    load_sem, send_sem, recv_sem, pick_send, pick_recv, len_send, len_recv,
):
    req = lax.axis_index("req")
    me = lax.axis_index("blk")
    slot = me // HEAD_DIVISIONS
    head_group = me % HEAD_DIVISIONS
    ring = SLOTS * HEAD_DIVISIONS
    right = (me + HEAD_DIVISIONS) % ring
    left = (me + ring - HEAD_DIVISIONS) % ring

    def quad_peer(e):
        low = head_group % 2
        high = head_group // 2
        if e & 1:
            low = 1 - low
        if e & 2:
            high = 1 - high
        return high * 2 + low

    core = req % 2
    y_low = (req // 2) % 2
    x = req // 4
    mate = req + 1 - 2 * core
    y_mate = req + 2 - 4 * y_low
    x_mates = [((x + i) % 4) * 4 + req % 4 for i in (1, 2, 3)]

    loads = [
        pltpu.make_async_copy(q_hbm, q_raw, load_sem.at[0]),
        pltpu.make_async_copy(k_hbm, kbuf.at[0], load_sem.at[1]),
        pltpu.make_async_copy(v_hbm, vbuf.at[0], load_sem.at[2]),
    ]
    for load in loads:
        load.start()

    barrier = pltpu.get_barrier_semaphore()
    partners = [(req, right), (req, left)]
    partners += [(req, slot * HEAD_DIVISIONS + quad_peer(e)) for e in (1, 2, 3)]
    partners += [(mate, me), (y_mate, me)] + [(xm, me) for xm in x_mates]
    for partner in partners:
        pl.semaphore_signal(barrier, inc=1, device_id=partner, device_id_type=MESH)
    pl.semaphore_wait(barrier, len(partners))

    def hop(side, turn, chunk):
        half = chunk // 2
        rows = pl.ds(half * BLOCK, BLOCK)
        is_value = chunk % 2 == 1
        buf = vbuf if is_value else kbuf
        if side == 0:
            source, target, device = turn, turn + 1, right
        else:
            source, target, device = (SLOTS - turn) % SLOTS, SLOTS - turn - 1, left
        if turn == 0:
            src = (v_hbm if is_value else k_hbm).at[rows]
        else:
            src = buf.at[source, rows]
        return pltpu.make_async_remote_copy(
            src_ref=src,
            dst_ref=buf.at[target, rows],
            send_sem=send_sem.at[side, turn, chunk],
            recv_sem=recv_sem.at[target, chunk],
            device_id=(req, device),
            device_id_type=MESH,
        )

    def travels(side, turn, chunk):
        if turn < 3:
            return True
        return turn == 3 and (chunk // 2 == side)

    sent = []
    for chunk in range(4):
        for side in range(2):
            copy = hop(side, 0, chunk)
            copy.start()
            sent.append(copy)

    lens[req] = jnp.full((8, 128), length_ref[0], jnp.int32)

    def len_copy(index, start, size, to):
        rows = lens.at[pl.ds(start, size)]
        return pltpu.make_async_remote_copy(
            src_ref=rows, dst_ref=rows, send_sem=len_send.at[index], recv_sem=len_recv.at[index],
            device_id=(to, me), device_id_type=MESH,
        )

    lane = lax.broadcasted_iota(jnp.int32, (BLOCK, HEAD), 1)
    row = lax.broadcasted_iota(jnp.int32, (BLOCK, HEAD), 0)
    pair = jnp.where(lane < HALF_TURN, lane, lane - HALF_TURN).astype(jnp.float32)
    frequency = jnp.exp(-math.log(ROPE_BASE) * (2.0 * pair) / HEAD)
    sign = jnp.where(lane < HALF_TURN, -1.0, 1.0)
    angle = row.astype(jnp.float32) * frequency
    cos_row[...] = jnp.cos(angle)
    sin_row[...] = jnp.sin(angle) * sign

    blk_row = lax.broadcasted_iota(jnp.int32, (2 * SLOTS, HEAD), 0)
    blk_of = jnp.zeros((2 * SLOTS, HEAD), jnp.int32)
    for s in range(SLOTS):
        for half in range(2):
            blk_of = jnp.where(blk_row == 2 * s + half, table[0, half, s], blk_of)
    base = (blk_of * BLOCK).astype(jnp.float32) * frequency[: 2 * SLOTS]
    cos_blk[...] = jnp.cos(base)
    sin_blk[...] = jnp.sin(base) * sign[: 2 * SLOTS]

    def turn_tables(source, half):
        at = pl.ds(2 * source + half, 1)
        cos_b = jnp.broadcast_to(cos_blk[at, :], (BLOCK, HEAD))
        sin_b = jnp.broadcast_to(sin_blk[at, :], (BLOCK, HEAD))
        cos_r, sin_r = cos_row[...], sin_row[...]
        return cos_b * cos_r - sin_b * sin_r, sin_b * cos_r + cos_b * sin_r

    def rotated(part, cosine, sine):
        part = part.astype(jnp.float32)
        return part * cosine + pltpu.roll(part, HALF_TURN, 1) * sine

    residue = []
    for h in range(HEAD_DIVISIONS):
        wanted = slot * HEAD_DIVISIONS + h
        found = jnp.int32(0)
        for r in range(RESIDUES):
            found = found + pick(rank_of[0, r] == wanted, r)
        residue.append(found)
    c_row = lax.broadcasted_iota(jnp.int32, (64, 2 * BLOCK), 0)
    c_col = lax.broadcasted_iota(jnp.int32, (64, 2 * BLOCK), 1)
    wanted_col = ((c_row % 16) // 8) * BLOCK + (c_row % 8) * RESIDUES
    for h in range(HEAD_DIVISIONS):
        wanted_col = wanted_col + pick(c_row // 16 == h, residue[h])
    choose[...] = jnp.where(c_col == wanted_col, 1.0, 0.0).astype(jnp.bfloat16)

    mate_copy = len_copy(0, req, 1, mate)
    mate_copy.start()
    sent.append(mate_copy)

    for load in loads:
        load.wait()

    q_block = [table[0, half, slot] for half in range(2)]
    own_low = jnp.minimum(q_block[0], q_block[1])
    first_low = q_block[0] < q_block[1]
    q_tables = [turn_tables(slot, half) for half in range(2)]
    for head in range(2 * KV_DEV):
        cols = slice(head * HEAD, (head + 1) * HEAD)
        turned = [rotated(q_raw[h * BLOCK : (h + 1) * BLOCK, cols], *q_tables[h]) * QUERY_SCALE for h in range(2)]
        at = (head % 2) * 2
        qrot[head // 2, at] = jnp.where(first_low, turned[0], turned[1]).astype(jnp.bfloat16)
        qrot[head // 2, at + 1] = jnp.where(first_low, turned[1], turned[0]).astype(jnp.bfloat16)
    num[...] = jnp.zeros_like(num)
    den[...] = jnp.zeros_like(den)

    tile_row = lax.broadcasted_iota(jnp.int32, (BLOCK, BLOCK), 0)
    tile_col = lax.broadcasted_iota(jnp.int32, (BLOCK, BLOCK), 1)

    def choose_rows(order, kind, load):
        for head in range(KV_DEV):
            rows = jnp.dot(choose[...], load(head), preferred_element_type=jnp.float32)
            rows = rows.astype(jnp.bfloat16)
            first = kind * KV_DEV * HEAD + head * HEAD
            for h in range(HEAD_DIVISIONS):
                chosen[h, order, :, first : first + HEAD] = rows[h * 16 : (h + 1) * 16]

    def prepare_keys(order):
        j = ORDER[order]
        source = (slot + SLOTS - j) % SLOTS
        for half in range(2):
            cosine, sine = turn_tables(source, half)
            rows = slice(half * BLOCK, (half + 1) * BLOCK)
            for head in range(KV_DEV):
                part = kbuf[j, rows, head * HEAD : (head + 1) * HEAD]
                krot[head, rows, :] = rotated(part, cosine, sine).astype(jnp.bfloat16)
        choose_rows(order, 0, lambda head: krot[head])
        place(order, lambda head, half: krot[head, half * BLOCK : (half + 1) * BLOCK, :], kpair)

    def prepare_values(order):
        j = ORDER[order]

        def rows_of(head, half):
            return vbuf[j, half * BLOCK : (half + 1) * BLOCK, head * HEAD : (head + 1) * HEAD]

        choose_rows(order, 1, lambda head: vbuf[j, :, head * HEAD : (head + 1) * HEAD])
        place(order, rows_of, vpair)

    def prepare(order):
        prepare_keys(order)
        prepare_values(order)

    def meeting(order):
        source = (slot + SLOTS - ORDER[order]) % SLOTS
        first, second = table[0, 0, source], table[0, 1, source]
        to_low = jnp.minimum(first, second) < own_low
        low_first = jnp.where(first < second, 1, 0)
        other_first = jnp.where(to_low, low_first, 1 - low_first)
        return low_first == 1, other_first == 1, to_low

    def place(order, rows_of, target):
        low_first, other_first, _ = meeting(order)
        if order == 0:
            other_first = jnp.logical_not(low_first)
        for head in range(KV_DEV):
            first, second = rows_of(head, 0), rows_of(head, 1)
            target[head, 0] = jnp.where(low_first, first, second)
            target[head, 1] = jnp.where(other_first, first, second)

    def weigh(q_part, k_part, masked=False):
        scores = lax.dot_general(
            q_part, k_part, (((1,), (1,)), ((), ())), preferred_element_type=jnp.float32
        )
        expo = jnp.exp(CAP * jnp.tanh(scores * (1.0 / CAP)))
        if masked:
            expo = jnp.where(tile_col <= tile_row, expo, 0.0)
        return expo.astype(jnp.bfloat16), expo[:, :HEAD] + expo[:, HEAD:]

    def blend(weight, v_part):
        return jnp.dot(weight, v_part, preferred_element_type=jnp.float32)

    def attend_own(head):
        def tile(g, carry):
            weight, part = weigh(qrot[head, 2 * g], kpair[head, 0], True)
            num[head, 2 * g] = blend(weight, vpair[head, 0])
            den[head, 2 * g] = part
            weight, part = weigh(qrot[head, 2 * g + 1], kpair[head, 0])
            weight2, part2 = weigh(qrot[head, 2 * g + 1], kpair[head, 1], True)
            num[head, 2 * g + 1] = blend(weight, vpair[head, 0]) + blend(weight2, vpair[head, 1])
            den[head, 2 * g + 1] = part + part2
            return carry

        lax.fori_loop(0, 2, tile, 0)

    def add_parts(total, head, g, to_low, always, either):
        total[head, 2 * g] += jnp.where(to_low, either, 0.0)
        total[head, 2 * g + 1] += always + jnp.where(to_low, 0.0, either)

    def attend(order, head):
        _, _, to_low = meeting(order)

        def tile(g, carry):
            lower, upper = qrot[head, 2 * g], qrot[head, 2 * g + 1]
            weight, part = weigh(upper, kpair[head, 0])
            weight2, part2 = weigh(jnp.where(to_low, lower, upper), kpair[head, 1])
            add_parts(den, head, g, to_low, part, part2)
            always = blend(weight, vpair[head, 0])
            either = blend(weight2, vpair[head, 1])
            add_parts(num, head, g, to_low, always, either)
            return carry

        lax.fori_loop(0, 2, tile, 0)

    def weigh_last(order, head):
        _, _, to_low = meeting(order)

        def tile(g, carry):
            lower, upper = qrot[head, 2 * g], qrot[head, 2 * g + 1]
            weight, part = weigh(upper, kpair[head, 0])
            weight2, part2 = weigh(jnp.where(to_low, lower, upper), kpair[head, 1])
            kept_weight[head, 2 * g] = weight
            kept_weight[head, 2 * g + 1] = weight2
            add_parts(den, head, g, to_low, part, part2)
            return carry

        lax.fori_loop(0, 2, tile, 0)

    def blend_last(order, head):
        _, _, to_low = meeting(order)

        def tile(g, carry):
            always = blend(kept_weight[head, 2 * g], vpair[head, 0])
            either = blend(kept_weight[head, 2 * g + 1], vpair[head, 1])
            add_parts(num, head, g, to_low, always, either)
            return carry

        lax.fori_loop(0, 2, tile, 0)

    def share(batch, first, count):
        for e in (1, 2, 3):
            peer = quad_peer(e)
            copy = pltpu.make_async_remote_copy(
                src_ref=chosen.at[peer, pl.ds(first, count)],
                dst_ref=arrived.at[e, pl.ds(first, count)],
                send_sem=pick_send.at[e, batch],
                recv_sem=pick_recv.at[e, batch],
                device_id=(req, slot * HEAD_DIVISIONS + peer),
                device_id_type=MESH,
            )
            copy.start()
            sent.append(copy)
            shares.append(copy)

    shares = []

    def own_keys_and_first():
        prepare(0)
        attend_own(0)

    def first_of(order):
        prepare(order)
        attend(order, 0)

    work = {
        1: [own_keys_and_first, lambda: attend_own(1), lambda: None, lambda: None],
        2: [lambda: first_of(1), lambda: attend(1, 1), lambda: first_of(2), lambda: attend(2, 1)],
        3: [lambda: first_of(3), lambda: attend(3, 1), lambda: first_of(4), lambda: attend(4, 1)],
    }
    for turn in range(1, 4):
        for chunk in range(4):
            for side in range(2):
                hop(side, turn - 1, chunk).wait_recv()
                if travels(side, turn, chunk):
                    copy = hop(side, turn, chunk)
                    copy.start()
                    sent.append(copy)
            if chunk == 0 and turn == 2:
                mate_copy.wait_recv()
                y_copy = len_copy(1, (req // 2) * 2, 2, y_mate)
                y_copy.start()
                sent.append(y_copy)
            if chunk == 0 and turn == 3:
                y_copy.wait_recv()
                x_copies = [len_copy(2 + i, (req // 4) * 4, 4, x_mates[i]) for i in range(3)]
                for copy in x_copies:
                    copy.start()
                    sent.append(copy)
                share(0, 0, 3)
            work[turn][chunk]()
    share(1, 3, 2)
    prepare(5)
    attend(5, 0)
    attend(5, 1)
    prepare(6)
    attend(6, 0)
    attend(6, 1)
    share(2, 5, 2)
    hop(0, 3, 0).wait_recv()
    hop(1, 3, 2).wait_recv()
    prepare_keys(7)
    weigh_last(7, 0)
    weigh_last(7, 1)
    hop(0, 3, 1).wait_recv()
    hop(1, 3, 3).wait_recv()
    prepare_values(7)
    blend_last(7, 0)
    share(3, 7, 1)
    blend_last(7, 1)

    for copy in x_copies:
        copy.wait_recv()
    length = jnp.zeros((8, 128), jnp.int32)
    for p in range(16):
        length = length + pick(group_of[p] == req, lens[p])
    length = length[0:1, :]

    for half in range(2):
        rows = slice(half * BLOCK, (half + 1) * BLOCK)
        live = row + q_block[half] * BLOCK < jnp.broadcast_to(length, (BLOCK, HEAD))
        lower_here = first_low if half == 0 else jnp.logical_not(first_low)
        for head in range(2 * KV_DEV):
            at = (head % 2) * 2
            parts = jnp.where(lower_here, den[head // 2, at], den[head // 2, at + 1])
            total = jnp.sum(parts, axis=1, keepdims=True)
            value = jnp.where(lower_here, num[head // 2, at], num[head // 2, at + 1]) / total
            out_ref[rows, head * HEAD : (head + 1) * HEAD] = jnp.where(live, value, 0.0).astype(jnp.bfloat16)

    own_residue = jnp.int32(0)
    for r in range(RESIDUES):
        own_residue = own_residue + pick(rank_of[0, r] == me, r)
    p_row = lax.broadcasted_iota(jnp.int32, (HEAD, HEAD), 0)
    p_col = lax.broadcasted_iota(jnp.int32, (HEAD, HEAD), 1)
    place = p_col % 8
    for order in range(8):
        source = (slot + SLOTS - ORDER[order]) % SLOTS
        for half in range(2):
            place = place + pick(p_col // 8 == 2 * order + half, table[0, half, source] * 8)
    kept = p_row * RESIDUES + own_residue < jnp.broadcast_to(length, (HEAD, HEAD))
    placed = jnp.where(jnp.logical_and(place == p_row, kept), 1.0, 0.0).astype(jnp.bfloat16)

    for copy in shares:
        copy.wait_recv()
    width = KV_DEV * HEAD
    for e in range(4):
        from_head = head_group if e == 0 else quad_peer(e)
        data = chosen[head_group] if e == 0 else arrived[e]
        data = data.reshape(8 * 16, 2 * width)
        moved = jnp.dot(placed, data, preferred_element_type=jnp.float32).astype(jnp.bfloat16)
        for kind in range(2):
            start = pl.multiple_of(kind * HEAD_DIVISIONS * width + from_head * width, width)
            cache_ref[:, pl.ds(start, width)] = moved[:, kind * width : (kind + 1) * width]

    for copy in sent:
        copy.wait_send()


def on_device(queries, keys, values, block_map, lengths, group_of_prompt, decode_rank):
    rows = queries.shape[2]
    wide, narrow = queries.shape[3], keys.shape[3]
    anywhere = pl.BlockSpec(memory_space=pltpu.HBM)
    scalars = pl.BlockSpec(memory_space=pltpu.SMEM)
    vmem = pl.BlockSpec(memory_space=pltpu.VMEM)
    dma = pltpu.SemaphoreType.DMA
    bf16, f32 = jnp.bfloat16, jnp.float32
    out, cache = pl.pallas_call(
        kernel,
        out_shape=(
            jax.ShapeDtypeStruct((rows, wide), bf16),
            jax.ShapeDtypeStruct((rows // HEAD_DIVISIONS, 2048), bf16),
        ),
        in_specs=[anywhere] * 3 + [scalars] * 4,
        out_specs=(vmem, vmem),
        scratch_shapes=[
            pltpu.VMEM((rows, wide), bf16),
            pltpu.VMEM((SLOTS, rows, narrow), bf16),
            pltpu.VMEM((SLOTS, rows, narrow), bf16),
            pltpu.VMEM((KV_DEV, 4, BLOCK, HEAD), bf16),
            pltpu.VMEM((KV_DEV, rows, HEAD), bf16),
            pltpu.VMEM((KV_DEV, 4, BLOCK, HEAD), f32),
            pltpu.VMEM((KV_DEV, 4, BLOCK, HEAD), f32),
            pltpu.VMEM((BLOCK, HEAD), f32),
            pltpu.VMEM((BLOCK, HEAD), f32),
            pltpu.VMEM((2 * SLOTS, HEAD), f32),
            pltpu.VMEM((2 * SLOTS, HEAD), f32),
            pltpu.VMEM((64, 2 * BLOCK), bf16),
            pltpu.VMEM((HEAD_DIVISIONS, SLOTS, 16, 2 * narrow), bf16),
            pltpu.VMEM((HEAD_DIVISIONS, SLOTS, 16, 2 * narrow), bf16),
            pltpu.VMEM((16, 8, 128), jnp.int32),
            pltpu.VMEM((KV_DEV, 2, BLOCK, HEAD), bf16),
            pltpu.VMEM((KV_DEV, 2, BLOCK, HEAD), bf16),
            pltpu.VMEM((KV_DEV, 4, BLOCK, BLOCK), bf16),
            dma((3,)),
            dma((2, 4, 4)),
            dma((SLOTS, 4)),
            dma((4, 4)),
            dma((4, 4)),
            dma((5,)),
            dma((5,)),
        ],
        compiler_params=pltpu.CompilerParams(collective_id=0, has_side_effects=True, vmem_limit_bytes=32 * 2**20),
    )(
        *[pltpu.with_memory_space_constraint(a, pltpu.HBM) for a in (
            queries.reshape(rows, wide), keys.reshape(rows, narrow), values.reshape(rows, narrow),
            jnp.swapaxes(block_map, 1, 2),
        )],
        lengths,
        *[pltpu.with_memory_space_constraint(a, pltpu.HBM) for a in (group_of_prompt, decode_rank)],
    )
    return out[None, None], cache[None]


def solution(mesh):
    placed = (
        P("req", "blk", None, None),
        P("req", "blk", None, None),
        P("req", "blk", None, None),
        P("req", None, None),
        P("req"),
        P(),
        P("req", None),
    )
    return jax.shard_map(
        on_device,
        mesh=mesh,
        in_specs=placed,
        out_specs=(P("req", "blk", None, None), P("req", "blk", None)),
        check_vma=False,
    )
```

```python
import functools
import math

import jax
import jax.numpy as jnp
from jax import lax
from jax.experimental import pallas as pl
from jax.experimental.pallas import tpu as pltpu
from jax.sharding import PartitionSpec as P

SLOTS = 8
HEAD_DIVISIONS = 4
KV_DEV = 2
HEAD = 128
HALF_TURN = 64
BLOCK = 256
RESIDUES = 32
CAP = 50.0
QUERY_SCALE = 1.0 / 12.0
ROPE_BASE = 10000.0
ORDER = (0, 1, 7, 2, 6, 3, 5, 4)
MESH = pl.DeviceIdType.MESH


def pick(condition, value):
    return jnp.where(condition, value, 0)


def kernel(
    q_hbm, k_hbm, v_hbm, table, length_ref, group_of, rank_of,
    out_ref, cache_ref,
    q_raw, kbuf, vbuf, qrot, krot, num, den, cos_row, sin_row, cos_blk, sin_blk,
    choose, chosen, arrived, lens, kpair, vpair, kept_weight,
    load_sem, send_sem, recv_sem, pick_send, pick_recv, len_send, len_recv,
):
    req = lax.axis_index("req")
    me = lax.axis_index("blk")
    slot = me // HEAD_DIVISIONS
    head_group = me % HEAD_DIVISIONS
    ring = SLOTS * HEAD_DIVISIONS
    right = (me + HEAD_DIVISIONS) % ring
    left = (me + ring - HEAD_DIVISIONS) % ring

    def quad_peer(e):
        low = head_group % 2
        high = head_group // 2
        if e & 1:
            low = 1 - low
        if e & 2:
            high = 1 - high
        return high * 2 + low

    parity = head_group // 2
    across = (slot + SLOTS - 1 + 2 * parity) % SLOTS

    core = req % 2
    y_low = (req // 2) % 2
    x = req // 4
    mate = req + 1 - 2 * core
    y_mate = req + 2 - 4 * y_low
    x_mates = [((x + i) % 4) * 4 + req % 4 for i in (1, 2, 3)]

    loads = [
        pltpu.make_async_copy(q_hbm, q_raw, load_sem.at[0]),
        pltpu.make_async_copy(k_hbm, kbuf.at[0], load_sem.at[1]),
        pltpu.make_async_copy(v_hbm, vbuf.at[0], load_sem.at[2]),
    ]
    for load in loads:
        load.start()

    barrier = pltpu.get_barrier_semaphore()
    partners = [(req, right), (req, left)]
    partners += [(req, slot * HEAD_DIVISIONS + quad_peer(e)) for e in (1, 2, 3)]
    partners += [(req, across * HEAD_DIVISIONS + quad_peer(e)) for e in (2, 3)]
    partners += [(mate, me), (y_mate, me)] + [(xm, me) for xm in x_mates]
    for partner in partners:
        pl.semaphore_signal(barrier, inc=1, device_id=partner, device_id_type=MESH)
    pl.semaphore_wait(barrier, len(partners))

    def hop(side, turn, chunk):
        half = chunk // 2
        rows = pl.ds(half * BLOCK, BLOCK)
        is_value = chunk % 2 == 1
        buf = vbuf if is_value else kbuf
        if side == 0:
            source, target, device = turn, turn + 1, right
        else:
            source, target, device = (SLOTS - turn) % SLOTS, SLOTS - turn - 1, left
        if turn == 0:
            src = (v_hbm if is_value else k_hbm).at[rows]
        else:
            src = buf.at[source, rows]
        return pltpu.make_async_remote_copy(
            src_ref=src,
            dst_ref=buf.at[target, rows],
            send_sem=send_sem.at[side, turn, chunk],
            recv_sem=recv_sem.at[target, chunk],
            device_id=(req, device),
            device_id_type=MESH,
        )

    def travels(side, turn, chunk):
        if turn < 3:
            return True
        return turn == 3 and (chunk // 2 == side)

    sent = []
    for place_in_line in range(4):
        for side in range(2):
            copy = hop(side, 0, (place_in_line + 2 * side) % 4)
            copy.start()
            sent.append(copy)

    lens[req] = jnp.full((8, 128), length_ref[0], jnp.int32)

    def len_copy(index, start, size, to):
        rows = lens.at[pl.ds(start, size)]
        return pltpu.make_async_remote_copy(
            src_ref=rows, dst_ref=rows, send_sem=len_send.at[index], recv_sem=len_recv.at[index],
            device_id=(to, me), device_id_type=MESH,
        )

    lane = lax.broadcasted_iota(jnp.int32, (BLOCK, HEAD), 1)
    row = lax.broadcasted_iota(jnp.int32, (BLOCK, HEAD), 0)
    pair = jnp.where(lane < HALF_TURN, lane, lane - HALF_TURN).astype(jnp.float32)
    frequency = jnp.exp(-math.log(ROPE_BASE) * (2.0 * pair) / HEAD)
    sign = jnp.where(lane < HALF_TURN, -1.0, 1.0)
    angle = row.astype(jnp.float32) * frequency
    cos_row[...] = jnp.cos(angle)
    sin_row[...] = jnp.sin(angle) * sign

    blk_row = lax.broadcasted_iota(jnp.int32, (2 * SLOTS, HEAD), 0)
    blk_of = jnp.zeros((2 * SLOTS, HEAD), jnp.int32)
    for s in range(SLOTS):
        for half in range(2):
            blk_of = jnp.where(blk_row == 2 * s + half, table[0, half, s], blk_of)
    base = (blk_of * BLOCK).astype(jnp.float32) * frequency[: 2 * SLOTS]
    cos_blk[...] = jnp.cos(base)
    sin_blk[...] = jnp.sin(base) * sign[: 2 * SLOTS]

    def turn_tables(source, half):
        at = pl.ds(2 * source + half, 1)
        cos_b = jnp.broadcast_to(cos_blk[at, :], (BLOCK, HEAD))
        sin_b = jnp.broadcast_to(sin_blk[at, :], (BLOCK, HEAD))
        cos_r, sin_r = cos_row[...], sin_row[...]
        return cos_b * cos_r - sin_b * sin_r, sin_b * cos_r + cos_b * sin_r

    def rotated(part, cosine, sine):
        part = part.astype(jnp.float32)
        return part * cosine + pltpu.roll(part, HALF_TURN, 1) * sine

    peers = [slot * HEAD_DIVISIONS + (head_group if e == 0 else quad_peer(e)) for e in range(4)]
    peers += [across * HEAD_DIVISIONS + quad_peer(e) for e in (2, 3)]
    residue = []
    for wanted in peers:
        found = jnp.int32(0)
        for r in range(RESIDUES):
            found = found + pick(rank_of[0, r] == wanted, r)
        residue.append(found)
    c_row = lax.broadcasted_iota(jnp.int32, (16 * len(peers), 2 * BLOCK), 0)
    c_col = lax.broadcasted_iota(jnp.int32, (16 * len(peers), 2 * BLOCK), 1)
    wanted_col = ((c_row % 16) // 8) * BLOCK + (c_row % 8) * RESIDUES
    for d in range(len(peers)):
        wanted_col = wanted_col + pick(c_row // 16 == d, residue[d])
    choose[...] = jnp.where(c_col == wanted_col, 1.0, 0.0).astype(jnp.bfloat16)

    mate_copy = len_copy(0, req, 1, mate)
    mate_copy.start()
    sent.append(mate_copy)

    for load in loads:
        load.wait()

    q_block = [table[0, half, slot] for half in range(2)]
    own_low = jnp.minimum(q_block[0], q_block[1])
    first_low = q_block[0] < q_block[1]
    q_tables = [turn_tables(slot, half) for half in range(2)]
    for head in range(2 * KV_DEV):
        cols = slice(head * HEAD, (head + 1) * HEAD)
        turned = [rotated(q_raw[h * BLOCK : (h + 1) * BLOCK, cols], *q_tables[h]) * QUERY_SCALE for h in range(2)]
        at = (head % 2) * 2
        qrot[head // 2, at] = jnp.where(first_low, turned[0], turned[1]).astype(jnp.bfloat16)
        qrot[head // 2, at + 1] = jnp.where(first_low, turned[1], turned[0]).astype(jnp.bfloat16)
    num[...] = jnp.zeros_like(num)
    den[...] = jnp.zeros_like(den)

    tile_row = lax.broadcasted_iota(jnp.int32, (BLOCK, BLOCK), 0)
    tile_col = lax.broadcasted_iota(jnp.int32, (BLOCK, BLOCK), 1)

    def shelf(j):
        return (j + 2) % SLOTS

    def choose_rows(order, kind, load):
        for head in range(KV_DEV):
            rows = jnp.dot(choose[...], load(head), preferred_element_type=jnp.float32)
            rows = rows.astype(jnp.bfloat16)
            first = kind * KV_DEV * HEAD + head * HEAD
            for d in range(6):
                chosen[d, shelf(ORDER[order]), :, first : first + HEAD] = rows[d * 16 : (d + 1) * 16]

    def prepare_keys(order):
        j = ORDER[order]
        source = (slot + SLOTS - j) % SLOTS
        for half in range(2):
            cosine, sine = turn_tables(source, half)
            rows = slice(half * BLOCK, (half + 1) * BLOCK)
            for head in range(KV_DEV):
                part = kbuf[j, rows, head * HEAD : (head + 1) * HEAD]
                krot[head, rows, :] = rotated(part, cosine, sine).astype(jnp.bfloat16)
        choose_rows(order, 0, lambda head: krot[head])
        place(order, lambda head, half: krot[head, half * BLOCK : (half + 1) * BLOCK, :], kpair)

    def prepare_values(order):
        j = ORDER[order]

        def rows_of(head, half):
            return vbuf[j, half * BLOCK : (half + 1) * BLOCK, head * HEAD : (head + 1) * HEAD]

        choose_rows(order, 1, lambda head: vbuf[j, :, head * HEAD : (head + 1) * HEAD])
        place(order, rows_of, vpair)

    def prepare(order):
        prepare_keys(order)
        prepare_values(order)

    def meeting(order):
        source = (slot + SLOTS - ORDER[order]) % SLOTS
        first, second = table[0, 0, source], table[0, 1, source]
        to_low = jnp.minimum(first, second) < own_low
        low_first = jnp.where(first < second, 1, 0)
        other_first = jnp.where(to_low, low_first, 1 - low_first)
        return low_first == 1, other_first == 1, to_low

    def place(order, rows_of, target):
        low_first, other_first, _ = meeting(order)
        if order == 0:
            other_first = jnp.logical_not(low_first)
        for head in range(KV_DEV):
            first, second = rows_of(head, 0), rows_of(head, 1)
            target[head, 0] = jnp.where(low_first, first, second)
            target[head, 1] = jnp.where(other_first, first, second)

    def weigh(q_part, k_part, masked=False):
        scores = lax.dot_general(
            q_part, k_part, (((1,), (1,)), ((), ())), preferred_element_type=jnp.float32
        )
        expo = jnp.exp(CAP * jnp.tanh(scores * (1.0 / CAP)))
        if masked:
            expo = jnp.where(tile_col <= tile_row, expo, 0.0)
        return expo.astype(jnp.bfloat16), expo[:, :HEAD] + expo[:, HEAD:]

    def blend(weight, v_part):
        return jnp.dot(weight, v_part, preferred_element_type=jnp.float32)

    def attend_own(head):
        def tile(g, carry):
            weight, part = weigh(qrot[head, 2 * g], kpair[head, 0], True)
            num[head, 2 * g] = blend(weight, vpair[head, 0])
            den[head, 2 * g] = part
            weight, part = weigh(qrot[head, 2 * g + 1], kpair[head, 0])
            weight2, part2 = weigh(qrot[head, 2 * g + 1], kpair[head, 1], True)
            num[head, 2 * g + 1] = blend(weight, vpair[head, 0]) + blend(weight2, vpair[head, 1])
            den[head, 2 * g + 1] = part + part2
            return carry

        lax.fori_loop(0, 2, tile, 0)

    def add_parts(total, head, g, to_low, always, either):
        total[head, 2 * g] += jnp.where(to_low, either, 0.0)
        total[head, 2 * g + 1] += always + jnp.where(to_low, 0.0, either)

    def attend(order, head):
        _, _, to_low = meeting(order)

        def tile(g, carry):
            lower, upper = qrot[head, 2 * g], qrot[head, 2 * g + 1]
            weight, part = weigh(upper, kpair[head, 0])
            weight2, part2 = weigh(jnp.where(to_low, lower, upper), kpair[head, 1])
            add_parts(den, head, g, to_low, part, part2)
            always = blend(weight, vpair[head, 0])
            either = blend(weight2, vpair[head, 1])
            add_parts(num, head, g, to_low, always, either)
            return carry

        lax.fori_loop(0, 2, tile, 0)

    def weigh_last(order, head):
        _, _, to_low = meeting(order)

        def tile(g, carry):
            lower, upper = qrot[head, 2 * g], qrot[head, 2 * g + 1]
            weight, part = weigh(upper, kpair[head, 0])
            weight2, part2 = weigh(jnp.where(to_low, lower, upper), kpair[head, 1])
            kept_weight[head, 2 * g] = weight
            kept_weight[head, 2 * g + 1] = weight2
            add_parts(den, head, g, to_low, part, part2)
            return carry

        lax.fori_loop(0, 2, tile, 0)

    def blend_last(order, head):
        _, _, to_low = meeting(order)

        def tile(g, carry):
            always = blend(kept_weight[head, 2 * g], vpair[head, 0])
            either = blend(kept_weight[head, 2 * g + 1], vpair[head, 1])
            add_parts(num, head, g, to_low, always, either)
            return carry

        lax.fori_loop(0, 2, tile, 0)

    def share(to, e, source_at, target_at, count):
        index = len(shares)
        copy = pltpu.make_async_remote_copy(
            src_ref=chosen.at[e + 2 if to else e, pl.ds(source_at, count)],
            dst_ref=arrived.at[e, pl.ds(target_at, count)],
            send_sem=pick_send.at[index],
            recv_sem=pick_recv.at[index],
            device_id=(req, peers[e + 2 if to else e]),
            device_id_type=MESH,
        )
        copy.start()
        sent.append(copy)
        shares.append(copy)

    shares = []

    def own_keys_and_first():
        prepare(0)
        attend_own(0)

    def first_of(order):
        prepare(order)
        attend(order, 0)

    work = {
        1: [own_keys_and_first, lambda: attend_own(1), lambda: None, lambda: None],
        2: [lambda: first_of(1), lambda: attend(1, 1), lambda: first_of(2), lambda: attend(2, 1)],
        3: [lambda: first_of(3), lambda: attend(3, 1), lambda: first_of(4), lambda: attend(4, 1)],
    }
    for turn in range(1, 4):
        for place_in_line in range(4):
            for side in range(2):
                chunk = (place_in_line + 2 * side) % 4
                hop(side, turn - 1, chunk).wait_recv()
                if travels(side, turn, chunk):
                    copy = hop(side, turn, chunk)
                    copy.start()
                    sent.append(copy)
            if place_in_line == 0 and turn == 2:
                mate_copy.wait_recv()
                y_copy = len_copy(1, (req // 2) * 2, 2, y_mate)
                y_copy.start()
                sent.append(y_copy)
            if place_in_line == 0 and turn == 3:
                y_copy.wait_recv()
                x_copies = [len_copy(2 + i, (req // 4) * 4, 4, x_mates[i]) for i in range(3)]
                for copy in x_copies:
                    copy.start()
                    sent.append(copy)
            work[turn][place_in_line]()
    share(0, 1, 0, 0, 5)
    for e in (2, 3):
        share(1, e, 2 - 2 * parity, 1, 2)
        share(0, e, 0, 0, 1)
    prepare(5)
    attend(5, 0)
    attend(5, 1)
    prepare(6)
    attend(6, 0)
    attend(6, 1)
    for e in (1, 2, 3):
        share(0, e, 5, 5, 1)
        share(0, e, 7, 7, 1)
    for e in (2, 3):
        share(1, e, 4 - 2 * parity, 3, 2)
    hop(0, 3, 0).wait_recv()
    hop(1, 3, 2).wait_recv()
    prepare_keys(7)
    weigh_last(7, 0)
    weigh_last(7, 1)
    hop(0, 3, 1).wait_recv()
    hop(1, 3, 3).wait_recv()
    prepare_values(7)
    blend_last(7, 0)
    for e in (1, 2, 3):
        share(0, e, 6, 6, 1)
    blend_last(7, 1)

    for copy in x_copies:
        copy.wait_recv()
    length = jnp.zeros((8, 128), jnp.int32)
    for p in range(16):
        length = length + pick(group_of[p] == req, lens[p])
    length = length[0:1, :]

    for half in range(2):
        rows = slice(half * BLOCK, (half + 1) * BLOCK)
        live = row + q_block[half] * BLOCK < jnp.broadcast_to(length, (BLOCK, HEAD))
        lower_here = first_low if half == 0 else jnp.logical_not(first_low)
        for head in range(2 * KV_DEV):
            at = (head % 2) * 2
            parts = jnp.where(lower_here, den[head // 2, at], den[head // 2, at + 1])
            total = jnp.sum(parts, axis=1, keepdims=True)
            value = jnp.where(lower_here, num[head // 2, at], num[head // 2, at + 1]) / total
            out_ref[rows, head * HEAD : (head + 1) * HEAD] = jnp.where(live, value, 0.0).astype(jnp.bfloat16)

    own_residue = jnp.int32(0)
    for r in range(RESIDUES):
        own_residue = own_residue + pick(rank_of[0, r] == me, r)
    p_row = lax.broadcasted_iota(jnp.int32, (HEAD, HEAD), 0)
    p_col = lax.broadcasted_iota(jnp.int32, (HEAD, HEAD), 1)
    place = p_col % 8
    for order in range(8):
        source = (slot + SLOTS - ORDER[order]) % SLOTS
        for half in range(2):
            here = p_col // 8 == 2 * shelf(ORDER[order]) + half
            place = place + pick(here, table[0, half, source] * 8)
    kept = p_row * RESIDUES + own_residue < jnp.broadcast_to(length, (HEAD, HEAD))
    placed = jnp.where(jnp.logical_and(place == p_row, kept), 1.0, 0.0).astype(jnp.bfloat16)

    for copy in shares:
        copy.wait_recv()
    width = KV_DEV * HEAD
    for e in range(4):
        from_head = head_group if e == 0 else quad_peer(e)
        data = chosen[0] if e == 0 else arrived[e]
        data = data.reshape(8 * 16, 2 * width)
        moved = jnp.dot(placed, data, preferred_element_type=jnp.float32).astype(jnp.bfloat16)
        for kind in range(2):
            start = pl.multiple_of(kind * HEAD_DIVISIONS * width + from_head * width, width)
            cache_ref[:, pl.ds(start, width)] = moved[:, kind * width : (kind + 1) * width]

    for copy in sent:
        copy.wait_send()


def put_out(out_ref, cache_ref, out_to, cache_to, sem):
    first = pltpu.make_async_copy(out_ref, out_to, sem.at[0])
    second = pltpu.make_async_copy(cache_ref, cache_to, sem.at[1])
    first.start()
    second.start()
    first.wait()
    second.wait()


def on_device(queries, keys, values, block_map, lengths, group_of_prompt, decode_rank):
    rows = queries.shape[2]
    wide, narrow = queries.shape[3], keys.shape[3]
    anywhere = pl.BlockSpec(memory_space=pltpu.HBM)
    scalars = pl.BlockSpec(memory_space=pltpu.SMEM)
    vmem = pl.BlockSpec(memory_space=pltpu.VMEM)
    dma = pltpu.SemaphoreType.DMA
    bf16, f32 = jnp.bfloat16, jnp.float32
    out, cache = pl.pallas_call(
        kernel,
        out_shape=(
            jax.ShapeDtypeStruct((rows, wide), bf16),
            jax.ShapeDtypeStruct((rows // HEAD_DIVISIONS, 2048), bf16),
        ),
        in_specs=[anywhere] * 3 + [scalars] * 4,
        out_specs=(vmem, vmem),
        scratch_shapes=[
            pltpu.VMEM((rows, wide), bf16),
            pltpu.VMEM((SLOTS, rows, narrow), bf16),
            pltpu.VMEM((SLOTS, rows, narrow), bf16),
            pltpu.VMEM((KV_DEV, 4, BLOCK, HEAD), bf16),
            pltpu.VMEM((KV_DEV, rows, HEAD), bf16),
            pltpu.VMEM((KV_DEV, 4, BLOCK, HEAD), f32),
            pltpu.VMEM((KV_DEV, 4, BLOCK, HEAD), f32),
            pltpu.VMEM((BLOCK, HEAD), f32),
            pltpu.VMEM((BLOCK, HEAD), f32),
            pltpu.VMEM((2 * SLOTS, HEAD), f32),
            pltpu.VMEM((2 * SLOTS, HEAD), f32),
            pltpu.VMEM((96, 2 * BLOCK), bf16),
            pltpu.VMEM((6, SLOTS, 16, 2 * narrow), bf16),
            pltpu.VMEM((HEAD_DIVISIONS, SLOTS, 16, 2 * narrow), bf16),
            pltpu.VMEM((16, 8, 128), jnp.int32),
            pltpu.VMEM((KV_DEV, 2, BLOCK, HEAD), bf16),
            pltpu.VMEM((KV_DEV, 2, BLOCK, HEAD), bf16),
            pltpu.VMEM((KV_DEV, 4, BLOCK, BLOCK), bf16),
            dma((3,)),
            dma((2, 4, 4)),
            dma((SLOTS, 4)),
            dma((16,)),
            dma((16,)),
            dma((5,)),
            dma((5,)),
        ],
        compiler_params=pltpu.CompilerParams(collective_id=0, has_side_effects=True, vmem_limit_bytes=32 * 2**20),
    )(
        *[pltpu.with_memory_space_constraint(a, pltpu.HBM) for a in (
            queries.reshape(rows, wide), keys.reshape(rows, narrow), values.reshape(rows, narrow),
            jnp.swapaxes(block_map, 1, 2),
        )],
        lengths,
        *[pltpu.with_memory_space_constraint(a, pltpu.HBM) for a in (group_of_prompt, decode_rank)],
    )
    out, cache = pl.pallas_call(
        put_out,
        out_shape=(jax.ShapeDtypeStruct(out.shape, bf16), jax.ShapeDtypeStruct(cache.shape, bf16)),
        in_specs=[pl.BlockSpec(memory_space=pltpu.VMEM)] * 2,
        compiler_params=pltpu.CompilerParams(vmem_limit_bytes=8 * 2**20),
        out_specs=(pl.BlockSpec(memory_space=pl.ANY),) * 2,
        scratch_shapes=[dma((2,))],
    )(out, cache)
    return out[None, None], cache[None]


def solution(mesh):
    placed = (
        P("req", "blk", None, None),
        P("req", "blk", None, None),
        P("req", "blk", None, None),
        P("req", None, None),
        P("req"),
        P(),
        P("req", None),
    )
    return jax.shard_map(
        on_device,
        mesh=mesh,
        in_specs=placed,
        out_specs=(P("req", "blk", None, None), P("req", "blk", None)),
        check_vma=False,
    )
```

```python
import functools
import math

import jax
import jax.numpy as jnp
from jax import lax
from jax.experimental import pallas as pl
from jax.experimental.pallas import tpu as pltpu
from jax.sharding import PartitionSpec as P

SLOTS = 8
HEAD_DIVISIONS = 4
KV_DEV = 2
HEAD = 128
HALF_TURN = 64
BLOCK = 256
RESIDUES = 32
CAP = 50.0
QUERY_SCALE = 1.0 / 12.0
ROPE_BASE = 10000.0
ORDER = (0, 1, 7, 2, 6, 3, 5, 4)
MESH = pl.DeviceIdType.MESH


def pick(condition, value):
    return jnp.where(condition, value, 0)


def kernel(
    q_hbm, k_hbm, v_hbm, table, length_ref, group_of, rank_of,
    out_ref, cache_ref,
    q_raw, kbuf, vbuf, qrot, krot, num, den, cos_row, sin_row, cos_blk, sin_blk,
    choose, chosen, arrived, lens, kpair, vpair, kept_weight,
    load_sem, send_sem, recv_sem, pick_send, pick_recv, len_send, len_recv,
):
    req = lax.axis_index("req")
    me = lax.axis_index("blk")
    slot = me // HEAD_DIVISIONS
    head_group = me % HEAD_DIVISIONS
    ring = SLOTS * HEAD_DIVISIONS
    right = (me + HEAD_DIVISIONS) % ring
    left = (me + ring - HEAD_DIVISIONS) % ring

    def quad_peer(e):
        low = head_group % 2
        high = head_group // 2
        if e & 1:
            low = 1 - low
        if e & 2:
            high = 1 - high
        return high * 2 + low

    parity = head_group // 2
    across = (slot + SLOTS - 1 + 2 * parity) % SLOTS

    core = req % 2
    y_low = (req // 2) % 2
    x = req // 4
    mate = req + 1 - 2 * core
    y_mate = req + 2 - 4 * y_low
    x_mates = [(x + 1 - 2 * (x % 2)) * 4 + req % 4, ((x + 2) % 4) * 4 + req % 4]

    loads = [
        pltpu.make_async_copy(q_hbm, q_raw, load_sem.at[0]),
        pltpu.make_async_copy(k_hbm, kbuf.at[0], load_sem.at[1]),
        pltpu.make_async_copy(v_hbm, vbuf.at[0], load_sem.at[2]),
    ]
    for load in loads:
        load.start()

    barrier = pltpu.get_barrier_semaphore()
    partners = [(req, right), (req, left)]
    partners += [(req, slot * HEAD_DIVISIONS + quad_peer(e)) for e in (1, 2, 3)]
    partners += [(req, across * HEAD_DIVISIONS + quad_peer(e)) for e in (2, 3)]
    partners += [(mate, me), (y_mate, me)] + [(xm, me) for xm in x_mates]
    for partner in partners:
        pl.semaphore_signal(barrier, inc=1, device_id=partner, device_id_type=MESH)
    pl.semaphore_wait(barrier, len(partners))

    def hop(side, turn, chunk):
        half = chunk // 2
        rows = pl.ds(half * BLOCK, BLOCK)
        is_value = chunk % 2 == 1
        buf = vbuf if is_value else kbuf
        if side == 0:
            source, target, device = turn, turn + 1, right
        else:
            source, target, device = (SLOTS - turn) % SLOTS, SLOTS - turn - 1, left
        if turn == 0:
            src = (v_hbm if is_value else k_hbm).at[rows]
        else:
            src = buf.at[source, rows]
        return pltpu.make_async_remote_copy(
            src_ref=src,
            dst_ref=buf.at[target, rows],
            send_sem=send_sem.at[side, turn, chunk],
            recv_sem=recv_sem.at[target, chunk],
            device_id=(req, device),
            device_id_type=MESH,
        )

    def travels(side, turn, chunk):
        if turn < 3:
            return True
        return turn == 3 and (chunk // 2 == side)

    sent = []
    for place_in_line in range(4):
        for side in range(2):
            copy = hop(side, 0, (place_in_line + 2 * side) % 4)
            copy.start()
            sent.append(copy)

    lens[req] = jnp.full((8, 128), length_ref[0], jnp.int32)

    def len_copy(index, start, size, to):
        rows = lens.at[pl.ds(start, size)]
        return pltpu.make_async_remote_copy(
            src_ref=rows, dst_ref=rows, send_sem=len_send.at[index], recv_sem=len_recv.at[index],
            device_id=(to, me), device_id_type=MESH,
        )

    lane = lax.broadcasted_iota(jnp.int32, (BLOCK, HEAD), 1)
    row = lax.broadcasted_iota(jnp.int32, (BLOCK, HEAD), 0)
    pair = jnp.where(lane < HALF_TURN, lane, lane - HALF_TURN).astype(jnp.float32)
    frequency = jnp.exp(-math.log(ROPE_BASE) * (2.0 * pair) / HEAD)
    sign = jnp.where(lane < HALF_TURN, -1.0, 1.0)
    angle = row.astype(jnp.float32) * frequency
    cos_row[...] = jnp.cos(angle)
    sin_row[...] = jnp.sin(angle) * sign

    blk_row = lax.broadcasted_iota(jnp.int32, (2 * SLOTS, HEAD), 0)
    blk_of = jnp.zeros((2 * SLOTS, HEAD), jnp.int32)
    for s in range(SLOTS):
        for half in range(2):
            blk_of = jnp.where(blk_row == 2 * s + half, table[0, half, s], blk_of)
    base = (blk_of * BLOCK).astype(jnp.float32) * frequency[: 2 * SLOTS]
    cos_blk[...] = jnp.cos(base)
    sin_blk[...] = jnp.sin(base) * sign[: 2 * SLOTS]

    def turn_tables(source, half):
        at = pl.ds(2 * source + half, 1)
        cos_b = jnp.broadcast_to(cos_blk[at, :], (BLOCK, HEAD))
        sin_b = jnp.broadcast_to(sin_blk[at, :], (BLOCK, HEAD))
        cos_r, sin_r = cos_row[...], sin_row[...]
        return cos_b * cos_r - sin_b * sin_r, sin_b * cos_r + cos_b * sin_r

    def rotated(part, cosine, sine):
        part = part.astype(jnp.float32)
        return part * cosine + pltpu.roll(part, HALF_TURN, 1) * sine

    peers = [slot * HEAD_DIVISIONS + (head_group if e == 0 else quad_peer(e)) for e in range(4)]
    peers += [across * HEAD_DIVISIONS + quad_peer(e) for e in (2, 3)]
    residue = []
    for wanted in peers:
        found = jnp.int32(0)
        for r in range(RESIDUES):
            found = found + pick(rank_of[0, r] == wanted, r)
        residue.append(found)
    c_row = lax.broadcasted_iota(jnp.int32, (16 * len(peers), 2 * BLOCK), 0)
    c_col = lax.broadcasted_iota(jnp.int32, (16 * len(peers), 2 * BLOCK), 1)
    wanted_col = ((c_row % 16) // 8) * BLOCK + (c_row % 8) * RESIDUES
    for d in range(len(peers)):
        wanted_col = wanted_col + pick(c_row // 16 == d, residue[d])
    choose[...] = jnp.where(c_col == wanted_col, 1.0, 0.0).astype(jnp.bfloat16)

    mate_copy = len_copy(0, req, 1, mate)
    mate_copy.start()
    sent.append(mate_copy)

    for load in loads:
        load.wait()

    q_block = [table[0, half, slot] for half in range(2)]
    own_low = jnp.minimum(q_block[0], q_block[1])
    first_low = q_block[0] < q_block[1]
    q_tables = [turn_tables(slot, half) for half in range(2)]
    for head in range(2 * KV_DEV):
        cols = slice(head * HEAD, (head + 1) * HEAD)
        turned = [rotated(q_raw[h * BLOCK : (h + 1) * BLOCK, cols], *q_tables[h]) * QUERY_SCALE for h in range(2)]
        at = (head % 2) * 2
        qrot[head // 2, at] = jnp.where(first_low, turned[0], turned[1]).astype(jnp.bfloat16)
        qrot[head // 2, at + 1] = jnp.where(first_low, turned[1], turned[0]).astype(jnp.bfloat16)
    num[...] = jnp.zeros_like(num)
    den[...] = jnp.zeros_like(den)

    tile_row = lax.broadcasted_iota(jnp.int32, (BLOCK, BLOCK), 0)
    tile_col = lax.broadcasted_iota(jnp.int32, (BLOCK, BLOCK), 1)

    def shelf(j):
        return (j + 2) % SLOTS

    def choose_rows(order, kind, load):
        for head in range(KV_DEV):
            rows = jnp.dot(choose[...], load(head), preferred_element_type=jnp.float32)
            rows = rows.astype(jnp.bfloat16)
            first = kind * KV_DEV * HEAD + head * HEAD
            for d in range(6):
                chosen[d, shelf(ORDER[order]), :, first : first + HEAD] = rows[d * 16 : (d + 1) * 16]

    def prepare_keys(order):
        j = ORDER[order]
        source = (slot + SLOTS - j) % SLOTS
        for half in range(2):
            cosine, sine = turn_tables(source, half)
            rows = slice(half * BLOCK, (half + 1) * BLOCK)
            for head in range(KV_DEV):
                part = kbuf[j, rows, head * HEAD : (head + 1) * HEAD]
                krot[head, rows, :] = rotated(part, cosine, sine).astype(jnp.bfloat16)
        choose_rows(order, 0, lambda head: krot[head])
        place(order, lambda head, half: krot[head, half * BLOCK : (half + 1) * BLOCK, :], kpair)

    def prepare_values(order):
        j = ORDER[order]

        def rows_of(head, half):
            return vbuf[j, half * BLOCK : (half + 1) * BLOCK, head * HEAD : (head + 1) * HEAD]

        choose_rows(order, 1, lambda head: vbuf[j, :, head * HEAD : (head + 1) * HEAD])
        place(order, rows_of, vpair)

    def prepare(order):
        prepare_keys(order)
        prepare_values(order)

    def meeting(order):
        source = (slot + SLOTS - ORDER[order]) % SLOTS
        first, second = table[0, 0, source], table[0, 1, source]
        to_low = jnp.minimum(first, second) < own_low
        low_first = jnp.where(first < second, 1, 0)
        other_first = jnp.where(to_low, low_first, 1 - low_first)
        return low_first == 1, other_first == 1, to_low

    def place(order, rows_of, target):
        low_first, other_first, _ = meeting(order)
        if order == 0:
            other_first = jnp.logical_not(low_first)
        for head in range(KV_DEV):
            first, second = rows_of(head, 0), rows_of(head, 1)
            target[head, 0] = jnp.where(low_first, first, second)
            target[head, 1] = jnp.where(other_first, first, second)

    def weigh(q_part, k_part, masked=False):
        scores = lax.dot_general(
            q_part, k_part, (((1,), (1,)), ((), ())), preferred_element_type=jnp.float32
        )
        expo = jnp.exp(CAP * jnp.tanh(scores * (1.0 / CAP)))
        if masked:
            expo = jnp.where(tile_col <= tile_row, expo, 0.0)
        return expo.astype(jnp.bfloat16), expo[:, :HEAD] + expo[:, HEAD:]

    def blend(weight, v_part):
        return jnp.dot(weight, v_part, preferred_element_type=jnp.float32)

    def attend_own(head):
        def tile(g, carry):
            weight, part = weigh(qrot[head, 2 * g], kpair[head, 0], True)
            num[head, 2 * g] = blend(weight, vpair[head, 0])
            den[head, 2 * g] = part
            weight, part = weigh(qrot[head, 2 * g + 1], kpair[head, 0])
            weight2, part2 = weigh(qrot[head, 2 * g + 1], kpair[head, 1], True)
            num[head, 2 * g + 1] = blend(weight, vpair[head, 0]) + blend(weight2, vpair[head, 1])
            den[head, 2 * g + 1] = part + part2
            return carry

        lax.fori_loop(0, 2, tile, 0)

    def add_parts(total, head, g, to_low, always, either):
        total[head, 2 * g] += jnp.where(to_low, either, 0.0)
        total[head, 2 * g + 1] += always + jnp.where(to_low, 0.0, either)

    def attend(order, head):
        _, _, to_low = meeting(order)

        def tile(g, carry):
            lower, upper = qrot[head, 2 * g], qrot[head, 2 * g + 1]
            weight, part = weigh(upper, kpair[head, 0])
            weight2, part2 = weigh(jnp.where(to_low, lower, upper), kpair[head, 1])
            add_parts(den, head, g, to_low, part, part2)
            always = blend(weight, vpair[head, 0])
            either = blend(weight2, vpair[head, 1])
            add_parts(num, head, g, to_low, always, either)
            return carry

        lax.fori_loop(0, 2, tile, 0)

    def weigh_last(order, head):
        _, _, to_low = meeting(order)

        def tile(g, carry):
            lower, upper = qrot[head, 2 * g], qrot[head, 2 * g + 1]
            weight, part = weigh(upper, kpair[head, 0])
            weight2, part2 = weigh(jnp.where(to_low, lower, upper), kpair[head, 1])
            kept_weight[head, 2 * g] = weight
            kept_weight[head, 2 * g + 1] = weight2
            add_parts(den, head, g, to_low, part, part2)
            return carry

        lax.fori_loop(0, 2, tile, 0)

    def blend_last(order, head):
        _, _, to_low = meeting(order)

        def tile(g, carry):
            always = blend(kept_weight[head, 2 * g], vpair[head, 0])
            either = blend(kept_weight[head, 2 * g + 1], vpair[head, 1])
            add_parts(num, head, g, to_low, always, either)
            return carry

        lax.fori_loop(0, 2, tile, 0)

    def share(to, e, source_at, target_at, count):
        index = len(shares)
        copy = pltpu.make_async_remote_copy(
            src_ref=chosen.at[e + 2 if to else e, pl.ds(source_at, count)],
            dst_ref=arrived.at[e, pl.ds(target_at, count)],
            send_sem=pick_send.at[index],
            recv_sem=pick_recv.at[index],
            device_id=(req, peers[e + 2 if to else e]),
            device_id_type=MESH,
        )
        copy.start()
        sent.append(copy)
        shares.append(copy)

    shares = []

    def own_keys_and_first():
        prepare(0)
        attend_own(0)

    def first_of(order):
        prepare(order)
        attend(order, 0)

    work = {
        1: [own_keys_and_first, lambda: attend_own(1), lambda: None, lambda: None],
        2: [lambda: first_of(1), lambda: attend(1, 1), lambda: first_of(2), lambda: attend(2, 1)],
        3: [lambda: first_of(3), lambda: attend(3, 1), lambda: first_of(4), lambda: attend(4, 1)],
    }
    for turn in range(1, 4):
        for place_in_line in range(4):
            for side in range(2):
                chunk = (place_in_line + 2 * side) % 4
                hop(side, turn - 1, chunk).wait_recv()
                if travels(side, turn, chunk):
                    copy = hop(side, turn, chunk)
                    copy.start()
                    sent.append(copy)
            if place_in_line == 0 and turn == 2:
                mate_copy.wait_recv()
                y_copy = len_copy(1, (req // 2) * 2, 2, y_mate)
                y_copy.start()
                sent.append(y_copy)
            if place_in_line == 0 and turn == 3:
                y_copy.wait_recv()
                x_copy = len_copy(2, (req // 4) * 4, 4, x_mates[0])
                x_copy.start()
                sent.append(x_copy)
            work[turn][place_in_line]()
    share(0, 1, 0, 0, 5)
    for e in (2, 3):
        share(1, e, 2 - 2 * parity, 1, 2)
        share(0, e, 0, 0, 1)
    x_copy.wait_recv()
    far_copy = len_copy(3, (req // 8) * 8, 8, x_mates[1])
    far_copy.start()
    sent.append(far_copy)
    prepare(5)
    attend(5, 0)
    attend(5, 1)
    prepare(6)
    attend(6, 0)
    attend(6, 1)
    for e in (1, 2, 3):
        share(0, e, 5, 5, 1)
        share(0, e, 7, 7, 1)
    for e in (2, 3):
        share(1, e, 4 - 2 * parity, 3, 2)
    hop(0, 3, 0).wait_recv()
    hop(1, 3, 2).wait_recv()
    prepare_keys(7)
    weigh_last(7, 0)
    weigh_last(7, 1)
    hop(0, 3, 1).wait_recv()
    hop(1, 3, 3).wait_recv()
    prepare_values(7)
    for e in (1, 2, 3):
        share(0, e, 6, 6, 1)
    blend_last(7, 0)
    blend_last(7, 1)

    far_copy.wait_recv()
    length = jnp.zeros((8, 128), jnp.int32)
    for p in range(16):
        length = length + pick(group_of[p] == req, lens[p])
    length = length[0:1, :]

    for half in range(2):
        rows = slice(half * BLOCK, (half + 1) * BLOCK)
        live = row + q_block[half] * BLOCK < jnp.broadcast_to(length, (BLOCK, HEAD))
        lower_here = first_low if half == 0 else jnp.logical_not(first_low)
        for head in range(2 * KV_DEV):
            at = (head % 2) * 2
            parts = jnp.where(lower_here, den[head // 2, at], den[head // 2, at + 1])
            total = jnp.sum(parts, axis=1, keepdims=True)
            value = jnp.where(lower_here, num[head // 2, at], num[head // 2, at + 1]) / total
            out_ref[rows, head * HEAD : (head + 1) * HEAD] = jnp.where(live, value, 0.0).astype(jnp.bfloat16)

    own_residue = jnp.int32(0)
    for r in range(RESIDUES):
        own_residue = own_residue + pick(rank_of[0, r] == me, r)
    p_row = lax.broadcasted_iota(jnp.int32, (HEAD, HEAD), 0)
    p_col = lax.broadcasted_iota(jnp.int32, (HEAD, HEAD), 1)
    place = p_col % 8
    for order in range(8):
        source = (slot + SLOTS - ORDER[order]) % SLOTS
        for half in range(2):
            here = p_col // 8 == 2 * shelf(ORDER[order]) + half
            place = place + pick(here, table[0, half, source] * 8)
    kept = p_row * RESIDUES + own_residue < jnp.broadcast_to(length, (HEAD, HEAD))
    placed = jnp.where(jnp.logical_and(place == p_row, kept), 1.0, 0.0).astype(jnp.bfloat16)

    for copy in shares:
        copy.wait_recv()
    width = KV_DEV * HEAD
    for e in range(4):
        from_head = head_group if e == 0 else quad_peer(e)
        data = chosen[0] if e == 0 else arrived[e]
        data = data.reshape(8 * 16, 2 * width)
        moved = jnp.dot(placed, data, preferred_element_type=jnp.float32).astype(jnp.bfloat16)
        for kind in range(2):
            start = pl.multiple_of(kind * HEAD_DIVISIONS * width + from_head * width, width)
            cache_ref[:, pl.ds(start, width)] = moved[:, kind * width : (kind + 1) * width]

    for copy in sent:
        copy.wait_send()


def put_out(out_ref, cache_ref, out_to, cache_to, sem):
    first = pltpu.make_async_copy(out_ref, out_to, sem.at[0])
    second = pltpu.make_async_copy(cache_ref, cache_to, sem.at[1])
    first.start()
    second.start()
    first.wait()
    second.wait()


def on_device(queries, keys, values, block_map, lengths, group_of_prompt, decode_rank):
    rows = queries.shape[2]
    wide, narrow = queries.shape[3], keys.shape[3]
    anywhere = pl.BlockSpec(memory_space=pltpu.HBM)
    scalars = pl.BlockSpec(memory_space=pltpu.SMEM)
    vmem = pl.BlockSpec(memory_space=pltpu.VMEM)
    dma = pltpu.SemaphoreType.DMA
    bf16, f32 = jnp.bfloat16, jnp.float32
    out, cache = pl.pallas_call(
        kernel,
        out_shape=(
            jax.ShapeDtypeStruct((rows, wide), bf16),
            jax.ShapeDtypeStruct((rows // HEAD_DIVISIONS, 2048), bf16),
        ),
        in_specs=[anywhere] * 3 + [scalars] * 4,
        out_specs=(vmem, vmem),
        scratch_shapes=[
            pltpu.VMEM((rows, wide), bf16),
            pltpu.VMEM((SLOTS, rows, narrow), bf16),
            pltpu.VMEM((SLOTS, rows, narrow), bf16),
            pltpu.VMEM((KV_DEV, 4, BLOCK, HEAD), bf16),
            pltpu.VMEM((KV_DEV, rows, HEAD), bf16),
            pltpu.VMEM((KV_DEV, 4, BLOCK, HEAD), f32),
            pltpu.VMEM((KV_DEV, 4, BLOCK, HEAD), f32),
            pltpu.VMEM((BLOCK, HEAD), f32),
            pltpu.VMEM((BLOCK, HEAD), f32),
            pltpu.VMEM((2 * SLOTS, HEAD), f32),
            pltpu.VMEM((2 * SLOTS, HEAD), f32),
            pltpu.VMEM((96, 2 * BLOCK), bf16),
            pltpu.VMEM((6, SLOTS, 16, 2 * narrow), bf16),
            pltpu.VMEM((HEAD_DIVISIONS, SLOTS, 16, 2 * narrow), bf16),
            pltpu.VMEM((16, 8, 128), jnp.int32),
            pltpu.VMEM((KV_DEV, 2, BLOCK, HEAD), bf16),
            pltpu.VMEM((KV_DEV, 2, BLOCK, HEAD), bf16),
            pltpu.VMEM((KV_DEV, 4, BLOCK, BLOCK), bf16),
            dma((3,)),
            dma((2, 4, 4)),
            dma((SLOTS, 4)),
            dma((16,)),
            dma((16,)),
            dma((4,)),
            dma((4,)),
        ],
        compiler_params=pltpu.CompilerParams(collective_id=0, has_side_effects=True, vmem_limit_bytes=32 * 2**20),
    )(
        *[pltpu.with_memory_space_constraint(a, pltpu.HBM) for a in (
            queries.reshape(rows, wide), keys.reshape(rows, narrow), values.reshape(rows, narrow),
            jnp.swapaxes(block_map, 1, 2),
        )],
        lengths,
        *[pltpu.with_memory_space_constraint(a, pltpu.HBM) for a in (group_of_prompt, decode_rank)],
    )
    out, cache = pl.pallas_call(
        put_out,
        out_shape=(jax.ShapeDtypeStruct(out.shape, bf16), jax.ShapeDtypeStruct(cache.shape, bf16)),
        in_specs=[pl.BlockSpec(memory_space=pltpu.VMEM)] * 2,
        compiler_params=pltpu.CompilerParams(vmem_limit_bytes=8 * 2**20),
        out_specs=(pl.BlockSpec(memory_space=pl.ANY),) * 2,
        scratch_shapes=[dma((2,))],
    )(out, cache)
    return out[None, None], cache[None]


def solution(mesh):
    placed = (
        P("req", "blk", None, None),
        P("req", "blk", None, None),
        P("req", "blk", None, None),
        P("req", None, None),
        P("req"),
        P(),
        P("req", None),
    )
    return jax.shard_map(
        on_device,
        mesh=mesh,
        in_specs=placed,
        out_specs=(P("req", "blk", None, None), P("req", "blk", None)),
        check_vma=False,
    )
```

```python
import functools
import math

import jax
import jax.numpy as jnp
from jax import lax
from jax.experimental import pallas as pl
from jax.experimental.pallas import tpu as pltpu
from jax.sharding import PartitionSpec as P

SLOTS = 8
HEAD_DIVISIONS = 4
KV_DEV = 2
HEAD = 128
HALF_TURN = 64
BLOCK = 256
RESIDUES = 32
CAP = 50.0
QUERY_SCALE = 1.0 / 12.0
ROPE_BASE = 10000.0
ORDER = (0, 1, 7, 2, 6, 3, 5, 4)
MESH = pl.DeviceIdType.MESH


def pick(condition, value):
    return jnp.where(condition, value, 0)


def kernel(
    q_hbm, k_hbm, v_hbm, table, length_ref, group_of, rank_of,
    out_ref, cache_ref,
    q_raw, kbuf, vbuf, qrot, krot, num, den, cos_row, sin_row, cos_blk, sin_blk,
    choose, chosen, arrived, lens, kpair, vpair, kept_weight,
    load_sem, send_sem, recv_sem, pick_send, pick_recv, len_send, len_recv,
):
    req = lax.axis_index("req")
    me = lax.axis_index("blk")
    slot = me // HEAD_DIVISIONS
    head_group = me % HEAD_DIVISIONS
    ring = SLOTS * HEAD_DIVISIONS
    right = (me + HEAD_DIVISIONS) % ring
    left = (me + ring - HEAD_DIVISIONS) % ring

    def quad_peer(e):
        low = head_group % 2
        high = head_group // 2
        if e & 1:
            low = 1 - low
        if e & 2:
            high = 1 - high
        return high * 2 + low

    parity = head_group // 2
    across = (slot + SLOTS - 1 + 2 * parity) % SLOTS

    core = req % 2
    y_low = (req // 2) % 2
    x = req // 4
    mate = req + 1 - 2 * core
    y_mate = req + 2 - 4 * y_low
    x_mates = [(x + 1 - 2 * (x % 2)) * 4 + req % 4, ((x + 2) % 4) * 4 + req % 4]

    loads = [
        pltpu.make_async_copy(q_hbm, q_raw, load_sem.at[0]),
        pltpu.make_async_copy(k_hbm, kbuf.at[0], load_sem.at[1]),
        pltpu.make_async_copy(v_hbm, vbuf.at[0], load_sem.at[2]),
    ]
    for load in loads:
        load.start()

    barrier = pltpu.get_barrier_semaphore()
    partners = [(req, right), (req, left)]
    partners += [(req, slot * HEAD_DIVISIONS + quad_peer(e)) for e in (1, 2, 3)]
    partners += [(req, across * HEAD_DIVISIONS + quad_peer(e)) for e in (2, 3)]
    partners += [(mate, me), (y_mate, me)] + [(xm, me) for xm in x_mates]
    for partner in partners:
        pl.semaphore_signal(barrier, inc=1, device_id=partner, device_id_type=MESH)
    pl.semaphore_wait(barrier, len(partners))

    def hop(side, turn, chunk):
        half = chunk // 2
        rows = pl.ds(half * BLOCK, BLOCK)
        is_value = chunk % 2 == 1
        buf = vbuf if is_value else kbuf
        if side == 0:
            source, target, device = turn, turn + 1, right
        else:
            source, target, device = (SLOTS - turn) % SLOTS, SLOTS - turn - 1, left
        if turn == 0:
            src = (v_hbm if is_value else k_hbm).at[rows]
        else:
            src = buf.at[source, rows]
        return pltpu.make_async_remote_copy(
            src_ref=src,
            dst_ref=buf.at[target, rows],
            send_sem=send_sem.at[side, turn, chunk],
            recv_sem=recv_sem.at[target, chunk],
            device_id=(req, device),
            device_id_type=MESH,
        )

    def travels(side, turn, chunk):
        if turn < 3:
            return True
        return turn == 3 and (chunk // 2 == side)

    sent = []
    for place_in_line in range(4):
        for side in range(2):
            copy = hop(side, 0, (place_in_line + 2 * side) % 4)
            copy.start()
            sent.append(copy)

    lens[req] = jnp.full((8, 128), length_ref[0], jnp.int32)

    def len_copy(index, start, size, to):
        rows = lens.at[pl.ds(start, size)]
        return pltpu.make_async_remote_copy(
            src_ref=rows, dst_ref=rows, send_sem=len_send.at[index], recv_sem=len_recv.at[index],
            device_id=(to, me), device_id_type=MESH,
        )

    lane = lax.broadcasted_iota(jnp.int32, (BLOCK, HEAD), 1)
    row = lax.broadcasted_iota(jnp.int32, (BLOCK, HEAD), 0)
    pair = jnp.where(lane < HALF_TURN, lane, lane - HALF_TURN).astype(jnp.float32)
    frequency = jnp.exp(-math.log(ROPE_BASE) * (2.0 * pair) / HEAD)
    sign = jnp.where(lane < HALF_TURN, -1.0, 1.0)
    angle = row.astype(jnp.float32) * frequency
    cos_row[...] = jnp.cos(angle)
    sin_row[...] = jnp.sin(angle) * sign

    blk_row = lax.broadcasted_iota(jnp.int32, (2 * SLOTS, HEAD), 0)
    blk_of = jnp.zeros((2 * SLOTS, HEAD), jnp.int32)
    for s in range(SLOTS):
        for half in range(2):
            blk_of = jnp.where(blk_row == 2 * s + half, table[0, half, s], blk_of)
    base = (blk_of * BLOCK).astype(jnp.float32) * frequency[: 2 * SLOTS]
    cos_blk[...] = jnp.cos(base)
    sin_blk[...] = jnp.sin(base) * sign[: 2 * SLOTS]

    def turn_tables(source, half):
        at = pl.ds(2 * source + half, 1)
        cos_b = jnp.broadcast_to(cos_blk[at, :], (BLOCK, HEAD))
        sin_b = jnp.broadcast_to(sin_blk[at, :], (BLOCK, HEAD))
        cos_r, sin_r = cos_row[...], sin_row[...]
        return cos_b * cos_r - sin_b * sin_r, sin_b * cos_r + cos_b * sin_r

    def rotated(part, cosine, sine):
        part = part.astype(jnp.float32)
        return part * cosine + pltpu.roll(part, HALF_TURN, 1) * sine

    peers = [slot * HEAD_DIVISIONS + (head_group if e == 0 else quad_peer(e)) for e in range(4)]
    peers += [across * HEAD_DIVISIONS + quad_peer(e) for e in (2, 3)]
    residue = []
    for wanted in peers:
        found = jnp.int32(0)
        for r in range(RESIDUES):
            found = found + pick(rank_of[0, r] == wanted, r)
        residue.append(found)
    c_row = lax.broadcasted_iota(jnp.int32, (16 * len(peers), 2 * BLOCK), 0)
    c_col = lax.broadcasted_iota(jnp.int32, (16 * len(peers), 2 * BLOCK), 1)
    wanted_col = ((c_row % 16) // 8) * BLOCK + (c_row % 8) * RESIDUES
    for d in range(len(peers)):
        wanted_col = wanted_col + pick(c_row // 16 == d, residue[d])
    choose[...] = jnp.where(c_col == wanted_col, 1.0, 0.0).astype(jnp.bfloat16)

    mate_copy = len_copy(0, req, 1, mate)
    mate_copy.start()
    sent.append(mate_copy)

    for load in loads:
        load.wait()

    q_block = [table[0, half, slot] for half in range(2)]
    own_low = jnp.minimum(q_block[0], q_block[1])
    first_low = q_block[0] < q_block[1]
    q_tables = [turn_tables(slot, half) for half in range(2)]
    for head in range(2 * KV_DEV):
        cols = slice(head * HEAD, (head + 1) * HEAD)
        turned = [rotated(q_raw[h * BLOCK : (h + 1) * BLOCK, cols], *q_tables[h]) * QUERY_SCALE for h in range(2)]
        at = (head % 2) * 2
        qrot[head // 2, at] = jnp.where(first_low, turned[0], turned[1]).astype(jnp.bfloat16)
        qrot[head // 2, at + 1] = jnp.where(first_low, turned[1], turned[0]).astype(jnp.bfloat16)
    num[...] = jnp.zeros_like(num)
    den[...] = jnp.zeros_like(den)

    tile_row = lax.broadcasted_iota(jnp.int32, (BLOCK, BLOCK), 0)
    tile_col = lax.broadcasted_iota(jnp.int32, (BLOCK, BLOCK), 1)

    def shelf(j):
        return (j + 2) % SLOTS

    def choose_rows(order, kind, load):
        for head in range(KV_DEV):
            rows = jnp.dot(choose[...], load(head), preferred_element_type=jnp.float32)
            rows = rows.astype(jnp.bfloat16)
            first = kind * KV_DEV * HEAD + head * HEAD
            for d in range(6):
                chosen[d, shelf(ORDER[order]), :, first : first + HEAD] = rows[d * 16 : (d + 1) * 16]

    def prepare_keys(order):
        j = ORDER[order]
        source = (slot + SLOTS - j) % SLOTS
        for half in range(2):
            cosine, sine = turn_tables(source, half)
            rows = slice(half * BLOCK, (half + 1) * BLOCK)
            for head in range(KV_DEV):
                part = kbuf[j, rows, head * HEAD : (head + 1) * HEAD]
                krot[head, rows, :] = rotated(part, cosine, sine).astype(jnp.bfloat16)
        choose_rows(order, 0, lambda head: krot[head])
        place(order, lambda head, half: krot[head, half * BLOCK : (half + 1) * BLOCK, :], kpair)

    def prepare_values(order):
        j = ORDER[order]

        def rows_of(head, half):
            return vbuf[j, half * BLOCK : (half + 1) * BLOCK, head * HEAD : (head + 1) * HEAD]

        choose_rows(order, 1, lambda head: vbuf[j, :, head * HEAD : (head + 1) * HEAD])
        place(order, rows_of, vpair)

    def prepare(order):
        prepare_keys(order)
        prepare_values(order)

    def meeting(order):
        source = (slot + SLOTS - ORDER[order]) % SLOTS
        first, second = table[0, 0, source], table[0, 1, source]
        to_low = jnp.minimum(first, second) < own_low
        low_first = jnp.where(first < second, 1, 0)
        other_first = jnp.where(to_low, low_first, 1 - low_first)
        return low_first == 1, other_first == 1, to_low

    def place(order, rows_of, target):
        low_first, other_first, _ = meeting(order)
        if order == 0:
            other_first = jnp.logical_not(low_first)
        for head in range(KV_DEV):
            first, second = rows_of(head, 0), rows_of(head, 1)
            target[head, 0] = jnp.where(low_first, first, second)
            target[head, 1] = jnp.where(other_first, first, second)

    def weigh(q_part, k_part, masked=False):
        scores = lax.dot_general(
            q_part, k_part, (((1,), (1,)), ((), ())), preferred_element_type=jnp.float32
        )
        expo = jnp.exp(CAP * jnp.tanh(scores * (1.0 / CAP)))
        if masked:
            expo = jnp.where(tile_col <= tile_row, expo, 0.0)
        return expo.astype(jnp.bfloat16), expo[:, :HEAD] + expo[:, HEAD:]

    def blend(weight, v_part):
        return jnp.dot(weight, v_part, preferred_element_type=jnp.float32)

    def attend_own(head):
        def tile(g, carry):
            weight, part = weigh(qrot[head, 2 * g], kpair[head, 0], True)
            num[head, 2 * g] = blend(weight, vpair[head, 0])
            den[head, 2 * g] = part
            weight, part = weigh(qrot[head, 2 * g + 1], kpair[head, 0])
            weight2, part2 = weigh(qrot[head, 2 * g + 1], kpair[head, 1], True)
            num[head, 2 * g + 1] = blend(weight, vpair[head, 0]) + blend(weight2, vpair[head, 1])
            den[head, 2 * g + 1] = part + part2
            return carry

        lax.fori_loop(0, 2, tile, 0)

    def add_parts(total, head, g, to_low, always, either):
        total[head, 2 * g] += jnp.where(to_low, either, 0.0)
        total[head, 2 * g + 1] += always + jnp.where(to_low, 0.0, either)

    def attend(order, head):
        _, _, to_low = meeting(order)

        def tile(g, carry):
            lower, upper = qrot[head, 2 * g], qrot[head, 2 * g + 1]
            weight, part = weigh(upper, kpair[head, 0])
            weight2, part2 = weigh(jnp.where(to_low, lower, upper), kpair[head, 1])
            add_parts(den, head, g, to_low, part, part2)
            always = blend(weight, vpair[head, 0])
            either = blend(weight2, vpair[head, 1])
            add_parts(num, head, g, to_low, always, either)
            return carry

        lax.fori_loop(0, 2, tile, 0)

    def weigh_last(order, head):
        _, _, to_low = meeting(order)

        def tile(g, carry):
            lower, upper = qrot[head, 2 * g], qrot[head, 2 * g + 1]
            weight, part = weigh(upper, kpair[head, 0])
            weight2, part2 = weigh(jnp.where(to_low, lower, upper), kpair[head, 1])
            kept_weight[head, 2 * g] = weight
            kept_weight[head, 2 * g + 1] = weight2
            add_parts(den, head, g, to_low, part, part2)
            return carry

        lax.fori_loop(0, 2, tile, 0)

    def blend_last(order, head):
        _, _, to_low = meeting(order)

        def tile(g, carry):
            always = blend(kept_weight[head, 2 * g], vpair[head, 0])
            either = blend(kept_weight[head, 2 * g + 1], vpair[head, 1])
            add_parts(num, head, g, to_low, always, either)
            return carry

        lax.fori_loop(0, 2, tile, 0)

    def share(to, e, source_at, target_at, count):
        index = len(shares)
        copy = pltpu.make_async_remote_copy(
            src_ref=chosen.at[e + 2 if to else e, pl.ds(source_at, count)],
            dst_ref=arrived.at[e, pl.ds(target_at, count)],
            send_sem=pick_send.at[index],
            recv_sem=pick_recv.at[index],
            device_id=(req, peers[e + 2 if to else e]),
            device_id_type=MESH,
        )
        copy.start()
        sent.append(copy)
        shares.append(copy)

    shares = []

    def own_keys_and_first():
        prepare(0)
        attend_own(0)

    def first_of(order):
        prepare(order)
        attend(order, 0)

    work = {
        1: [own_keys_and_first, lambda: attend_own(1), lambda: None, lambda: None],
        2: [lambda: first_of(1), lambda: attend(1, 1), lambda: first_of(2), lambda: attend(2, 1)],
        3: [lambda: first_of(3), lambda: attend(3, 1), lambda: first_of(4), lambda: attend(4, 1)],
    }
    for turn in range(1, 4):
        for place_in_line in range(4):
            for side in range(2):
                chunk = (place_in_line + 2 * side) % 4
                hop(side, turn - 1, chunk).wait_recv()
                if travels(side, turn, chunk):
                    copy = hop(side, turn, chunk)
                    copy.start()
                    sent.append(copy)
            if place_in_line == 0 and turn == 2:
                mate_copy.wait_recv()
                y_copy = len_copy(1, (req // 2) * 2, 2, y_mate)
                y_copy.start()
                sent.append(y_copy)
            if place_in_line == 0 and turn == 3:
                y_copy.wait_recv()
                x_copy = len_copy(2, (req // 4) * 4, 4, x_mates[0])
                x_copy.start()
                sent.append(x_copy)
            work[turn][place_in_line]()
    share(0, 1, 0, 0, 5)
    for e in (2, 3):
        share(1, e, 2 - 2 * parity, 1, 2)
        share(0, e, 0, 0, 1)
    x_copy.wait_recv()
    far_copy = len_copy(3, (req // 8) * 8, 8, x_mates[1])
    far_copy.start()
    sent.append(far_copy)
    prepare(5)
    attend(5, 0)
    attend(5, 1)
    prepare(6)
    attend(6, 0)
    attend(6, 1)
    for e in (1, 2, 3):
        share(0, e, 5, 5, 1)
        share(0, e, 7, 7, 1)
    for e in (2, 3):
        share(1, e, 4 - 2 * parity, 3, 2)
    hop(0, 3, 0).wait_recv()
    hop(1, 3, 2).wait_recv()
    prepare_keys(7)
    weigh_last(7, 0)
    weigh_last(7, 1)
    hop(0, 3, 1).wait_recv()
    hop(1, 3, 3).wait_recv()
    prepare_values(7)
    for e in (1, 2, 3):
        share(0, e, 6, 6, 1)
    blend_last(7, 0)
    blend_last(7, 1)

    far_copy.wait_recv()
    length = jnp.zeros((8, 128), jnp.int32)
    for p in range(16):
        length = length + pick(group_of[p] == req, lens[p])
    length = length[0:1, :]

    for half in range(2):
        rows = slice(half * BLOCK, (half + 1) * BLOCK)
        live = row + q_block[half] * BLOCK < jnp.broadcast_to(length, (BLOCK, HEAD))
        lower_here = first_low if half == 0 else jnp.logical_not(first_low)
        for head in range(2 * KV_DEV):
            at = (head % 2) * 2
            parts = jnp.where(lower_here, den[head // 2, at], den[head // 2, at + 1])
            total = jnp.sum(parts, axis=1, keepdims=True)
            value = jnp.where(lower_here, num[head // 2, at], num[head // 2, at + 1]) / total
            out_ref[rows, head * HEAD : (head + 1) * HEAD] = jnp.where(live, value, 0.0).astype(jnp.bfloat16)

    own_residue = jnp.int32(0)
    for r in range(RESIDUES):
        own_residue = own_residue + pick(rank_of[0, r] == me, r)
    p_row = lax.broadcasted_iota(jnp.int32, (HEAD, HEAD), 0)
    p_col = lax.broadcasted_iota(jnp.int32, (HEAD, HEAD), 1)
    place = p_col % 8
    for order in range(8):
        source = (slot + SLOTS - ORDER[order]) % SLOTS
        for half in range(2):
            here = p_col // 8 == 2 * shelf(ORDER[order]) + half
            place = place + pick(here, table[0, half, source] * 8)
    kept = p_row * RESIDUES + own_residue < jnp.broadcast_to(length, (HEAD, HEAD))
    placed = jnp.where(jnp.logical_and(place == p_row, kept), 1.0, 0.0).astype(jnp.bfloat16)

    for copy in shares:
        copy.wait_recv()
    width = KV_DEV * HEAD
    for e in range(4):
        from_head = head_group if e == 0 else quad_peer(e)
        data = chosen[0] if e == 0 else arrived[e]
        data = data.reshape(8 * 16, 2 * width)
        moved = jnp.dot(placed, data, preferred_element_type=jnp.float32).astype(jnp.bfloat16)
        for kind in range(2):
            start = pl.multiple_of(kind * HEAD_DIVISIONS * width + from_head * width, width)
            cache_ref[:, pl.ds(start, width)] = moved[:, kind * width : (kind + 1) * width]

    for copy in sent:
        copy.wait_send()


PIECES = 4


def put_out(out_ref, cache_ref, out_to, cache_to, sem):
    copies = []
    for which, (source, target) in enumerate(((out_ref, out_to), (cache_ref, cache_to))):
        size = source.shape[0] // PIECES
        for piece in range(PIECES):
            rows = pl.ds(piece * size, size)
            copies.append(pltpu.make_async_copy(source.at[rows], target.at[rows], sem.at[which, piece]))
    for copy in copies:
        copy.start()
    for copy in copies:
        copy.wait()


def on_device(queries, keys, values, block_map, lengths, group_of_prompt, decode_rank):
    rows = queries.shape[2]
    wide, narrow = queries.shape[3], keys.shape[3]
    anywhere = pl.BlockSpec(memory_space=pltpu.HBM)
    scalars = pl.BlockSpec(memory_space=pltpu.SMEM)
    vmem = pl.BlockSpec(memory_space=pltpu.VMEM)
    dma = pltpu.SemaphoreType.DMA
    bf16, f32 = jnp.bfloat16, jnp.float32
    out, cache = pl.pallas_call(
        kernel,
        out_shape=(
            jax.ShapeDtypeStruct((rows, wide), bf16),
            jax.ShapeDtypeStruct((rows // HEAD_DIVISIONS, 2048), bf16),
        ),
        in_specs=[anywhere] * 3 + [scalars] * 4,
        out_specs=(vmem, vmem),
        scratch_shapes=[
            pltpu.VMEM((rows, wide), bf16),
            pltpu.VMEM((SLOTS, rows, narrow), bf16),
            pltpu.VMEM((SLOTS, rows, narrow), bf16),
            pltpu.VMEM((KV_DEV, 4, BLOCK, HEAD), bf16),
            pltpu.VMEM((KV_DEV, rows, HEAD), bf16),
            pltpu.VMEM((KV_DEV, 4, BLOCK, HEAD), f32),
            pltpu.VMEM((KV_DEV, 4, BLOCK, HEAD), f32),
            pltpu.VMEM((BLOCK, HEAD), f32),
            pltpu.VMEM((BLOCK, HEAD), f32),
            pltpu.VMEM((2 * SLOTS, HEAD), f32),
            pltpu.VMEM((2 * SLOTS, HEAD), f32),
            pltpu.VMEM((96, 2 * BLOCK), bf16),
            pltpu.VMEM((6, SLOTS, 16, 2 * narrow), bf16),
            pltpu.VMEM((HEAD_DIVISIONS, SLOTS, 16, 2 * narrow), bf16),
            pltpu.VMEM((16, 8, 128), jnp.int32),
            pltpu.VMEM((KV_DEV, 2, BLOCK, HEAD), bf16),
            pltpu.VMEM((KV_DEV, 2, BLOCK, HEAD), bf16),
            pltpu.VMEM((KV_DEV, 4, BLOCK, BLOCK), bf16),
            dma((3,)),
            dma((2, 4, 4)),
            dma((SLOTS, 4)),
            dma((16,)),
            dma((16,)),
            dma((4,)),
            dma((4,)),
        ],
        compiler_params=pltpu.CompilerParams(collective_id=0, has_side_effects=True, vmem_limit_bytes=32 * 2**20),
    )(
        *[pltpu.with_memory_space_constraint(a, pltpu.HBM) for a in (
            queries.reshape(rows, wide), keys.reshape(rows, narrow), values.reshape(rows, narrow),
            jnp.swapaxes(block_map, 1, 2),
        )],
        lengths,
        *[pltpu.with_memory_space_constraint(a, pltpu.HBM) for a in (group_of_prompt, decode_rank)],
    )
    out, cache = pl.pallas_call(
        put_out,
        out_shape=(jax.ShapeDtypeStruct(out.shape, bf16), jax.ShapeDtypeStruct(cache.shape, bf16)),
        in_specs=[pl.BlockSpec(memory_space=pltpu.VMEM)] * 2,
        compiler_params=pltpu.CompilerParams(vmem_limit_bytes=8 * 2**20),
        out_specs=(pl.BlockSpec(memory_space=pl.ANY),) * 2,
        scratch_shapes=[dma((2, PIECES))],
    )(out, cache)
    return out[None, None], cache[None]


def solution(mesh):
    placed = (
        P("req", "blk", None, None),
        P("req", "blk", None, None),
        P("req", "blk", None, None),
        P("req", None, None),
        P("req"),
        P(),
        P("req", None),
    )
    return jax.shard_map(
        on_device,
        mesh=mesh,
        in_specs=placed,
        out_specs=(P("req", "blk", None, None), P("req", "blk", None)),
        check_vma=False,
    )
```

```python
import functools
import math

import jax
import jax.numpy as jnp
from jax import lax
from jax.experimental import pallas as pl
from jax.experimental.pallas import tpu as pltpu
from jax.sharding import PartitionSpec as P

SLOTS = 8
HEAD_DIVISIONS = 4
KV_DEV = 2
HEAD = 128
HALF_TURN = 64
BLOCK = 256
RESIDUES = 32
CAP = 50.0
QUERY_SCALE = 1.0 / 12.0
ROPE_BASE = 10000.0
DEPTH = 3
ORDER = (0, 1, 7, 2, 6, 3, 5, 4)
MESH = pl.DeviceIdType.MESH


def pick(condition, value):
    return jnp.where(condition, value, 0)


def kernel(
    q_hbm, k_hbm, v_hbm, table, length_ref, group_of, rank_of,
    out_ref, cache_ref,
    q_raw, kbuf, vbuf, qrot, krot, num, den, cos_row, sin_row, cos_blk, sin_blk,
    choose, chosen, arrived, lens, kpair, vpair, kept_weight,
    load_sem, send_sem, recv_sem, pick_send, pick_recv, len_send, len_recv,
):
    req = lax.axis_index("req")
    me = lax.axis_index("blk")
    slot = me // HEAD_DIVISIONS
    head_group = me % HEAD_DIVISIONS
    ring = SLOTS * HEAD_DIVISIONS
    right = (me + HEAD_DIVISIONS) % ring
    left = (me + ring - HEAD_DIVISIONS) % ring

    def quad_peer(e):
        low = head_group % 2
        high = head_group // 2
        if e & 1:
            low = 1 - low
        if e & 2:
            high = 1 - high
        return high * 2 + low

    parity = head_group // 2
    across = (slot + SLOTS - 1 + 2 * parity) % SLOTS

    core = req % 2
    y_low = (req // 2) % 2
    x = req // 4
    mate = req + 1 - 2 * core
    y_mate = req + 2 - 4 * y_low
    x_mates = [((x + i) % 4) * 4 + req % 4 for i in (1, 2, 3)]

    loads = [
        pltpu.make_async_copy(q_hbm, q_raw, load_sem.at[0]),
        pltpu.make_async_copy(k_hbm, kbuf.at[0], load_sem.at[1]),
        pltpu.make_async_copy(v_hbm, vbuf.at[0], load_sem.at[2]),
    ]
    for load in loads:
        load.start()

    barrier = pltpu.get_barrier_semaphore()
    partners = [(req, right), (req, left)]
    partners += [(req, slot * HEAD_DIVISIONS + quad_peer(e)) for e in (1, 2, 3)]
    partners += [(req, across * HEAD_DIVISIONS + quad_peer(e)) for e in (2, 3)]
    partners += [(mate, me), (y_mate, me)] + [(xm, me) for xm in x_mates]
    for partner in partners:
        pl.semaphore_signal(barrier, inc=1, device_id=partner, device_id_type=MESH)
    pl.semaphore_wait(barrier, len(partners))

    def hop(side, turn, chunk):
        half = chunk // 2
        rows = pl.ds(half * BLOCK, BLOCK)
        is_value = chunk % 2 == 1
        buf = vbuf if is_value else kbuf
        if side == 0:
            source, target, device = turn, turn + 1, right
        else:
            source, target, device = (SLOTS - turn) % SLOTS, SLOTS - turn - 1, left
        if turn == 0:
            src = (v_hbm if is_value else k_hbm).at[rows]
        else:
            src = buf.at[source, rows]
        return pltpu.make_async_remote_copy(
            src_ref=src,
            dst_ref=buf.at[target, rows],
            send_sem=send_sem.at[side, turn, chunk],
            recv_sem=recv_sem.at[target, chunk],
            device_id=(req, device),
            device_id_type=MESH,
        )

    line = [[(step // 4, (step % 4 + 2 * side) % 4) for step in range(14)] for side in range(2)]
    copies = [[hop(side, *line[side][step]) for step in range(14)] for side in range(2)]
    for step in range(DEPTH):
        for side in range(2):
            copies[side][step].start()
    sent = []

    lens[req] = jnp.full((8, 128), length_ref[0], jnp.int32)

    def len_copy(index, start, size, to):
        rows = lens.at[pl.ds(start, size)]
        return pltpu.make_async_remote_copy(
            src_ref=rows, dst_ref=rows, send_sem=len_send.at[index], recv_sem=len_recv.at[index],
            device_id=(to, me), device_id_type=MESH,
        )

    lane = lax.broadcasted_iota(jnp.int32, (BLOCK, HEAD), 1)
    row = lax.broadcasted_iota(jnp.int32, (BLOCK, HEAD), 0)
    pair = jnp.where(lane < HALF_TURN, lane, lane - HALF_TURN).astype(jnp.float32)
    frequency = jnp.exp(-math.log(ROPE_BASE) * (2.0 * pair) / HEAD)
    sign = jnp.where(lane < HALF_TURN, -1.0, 1.0)
    angle = row.astype(jnp.float32) * frequency
    cos_row[...] = jnp.cos(angle)
    sin_row[...] = jnp.sin(angle) * sign

    blk_row = lax.broadcasted_iota(jnp.int32, (2 * SLOTS, HEAD), 0)
    blk_of = jnp.zeros((2 * SLOTS, HEAD), jnp.int32)
    for s in range(SLOTS):
        for half in range(2):
            blk_of = jnp.where(blk_row == 2 * s + half, table[0, half, s], blk_of)
    base = (blk_of * BLOCK).astype(jnp.float32) * frequency[: 2 * SLOTS]
    cos_blk[...] = jnp.cos(base)
    sin_blk[...] = jnp.sin(base) * sign[: 2 * SLOTS]

    def turn_tables(source, half):
        at = pl.ds(2 * source + half, 1)
        cos_b = jnp.broadcast_to(cos_blk[at, :], (BLOCK, HEAD))
        sin_b = jnp.broadcast_to(sin_blk[at, :], (BLOCK, HEAD))
        cos_r, sin_r = cos_row[...], sin_row[...]
        return cos_b * cos_r - sin_b * sin_r, sin_b * cos_r + cos_b * sin_r

    def rotated(part, cosine, sine):
        part = part.astype(jnp.float32)
        return part * cosine + pltpu.roll(part, HALF_TURN, 1) * sine

    peers = [slot * HEAD_DIVISIONS + (head_group if e == 0 else quad_peer(e)) for e in range(4)]
    peers += [across * HEAD_DIVISIONS + quad_peer(e) for e in (2, 3)]
    residue = []
    for wanted in peers:
        found = jnp.int32(0)
        for r in range(RESIDUES):
            found = found + pick(rank_of[0, r] == wanted, r)
        residue.append(found)
    c_row = lax.broadcasted_iota(jnp.int32, (16 * len(peers), 2 * BLOCK), 0)
    c_col = lax.broadcasted_iota(jnp.int32, (16 * len(peers), 2 * BLOCK), 1)
    wanted_col = ((c_row % 16) // 8) * BLOCK + (c_row % 8) * RESIDUES
    for d in range(len(peers)):
        wanted_col = wanted_col + pick(c_row // 16 == d, residue[d])
    choose[...] = jnp.where(c_col == wanted_col, 1.0, 0.0).astype(jnp.bfloat16)

    mate_copy = len_copy(0, req, 1, mate)
    mate_copy.start()
    sent.append(mate_copy)

    for load in loads:
        load.wait()

    q_block = [table[0, half, slot] for half in range(2)]
    own_low = jnp.minimum(q_block[0], q_block[1])
    first_low = q_block[0] < q_block[1]
    q_tables = [turn_tables(slot, half) for half in range(2)]
    for head in range(2 * KV_DEV):
        cols = slice(head * HEAD, (head + 1) * HEAD)
        turned = [rotated(q_raw[h * BLOCK : (h + 1) * BLOCK, cols], *q_tables[h]) * QUERY_SCALE for h in range(2)]
        at = (head % 2) * 2
        qrot[head // 2, at] = jnp.where(first_low, turned[0], turned[1]).astype(jnp.bfloat16)
        qrot[head // 2, at + 1] = jnp.where(first_low, turned[1], turned[0]).astype(jnp.bfloat16)
    num[...] = jnp.zeros_like(num)
    den[...] = jnp.zeros_like(den)

    tile_row = lax.broadcasted_iota(jnp.int32, (BLOCK, BLOCK), 0)
    tile_col = lax.broadcasted_iota(jnp.int32, (BLOCK, BLOCK), 1)

    def shelf(j):
        return (j + 2) % SLOTS

    def choose_rows(order, kind, load):
        for head in range(KV_DEV):
            rows = jnp.dot(choose[...], load(head), preferred_element_type=jnp.float32)
            rows = rows.astype(jnp.bfloat16)
            first = kind * KV_DEV * HEAD + head * HEAD
            for d in range(6):
                chosen[d, shelf(ORDER[order]), :, first : first + HEAD] = rows[d * 16 : (d + 1) * 16]

    def prepare_keys(order):
        j = ORDER[order]
        source = (slot + SLOTS - j) % SLOTS
        for half in range(2):
            cosine, sine = turn_tables(source, half)
            rows = slice(half * BLOCK, (half + 1) * BLOCK)
            for head in range(KV_DEV):
                part = kbuf[j, rows, head * HEAD : (head + 1) * HEAD]
                krot[head, rows, :] = rotated(part, cosine, sine).astype(jnp.bfloat16)
        choose_rows(order, 0, lambda head: krot[head])
        place(order, lambda head, half: krot[head, half * BLOCK : (half + 1) * BLOCK, :], kpair)

    def prepare_values(order):
        j = ORDER[order]

        def rows_of(head, half):
            return vbuf[j, half * BLOCK : (half + 1) * BLOCK, head * HEAD : (head + 1) * HEAD]

        choose_rows(order, 1, lambda head: vbuf[j, :, head * HEAD : (head + 1) * HEAD])
        place(order, rows_of, vpair)

    def prepare(order):
        prepare_keys(order)
        prepare_values(order)

    def meeting(order):
        source = (slot + SLOTS - ORDER[order]) % SLOTS
        first, second = table[0, 0, source], table[0, 1, source]
        to_low = jnp.minimum(first, second) < own_low
        low_first = jnp.where(first < second, 1, 0)
        other_first = jnp.where(to_low, low_first, 1 - low_first)
        return low_first == 1, other_first == 1, to_low

    def place(order, rows_of, target):
        low_first, other_first, _ = meeting(order)
        if order == 0:
            other_first = jnp.logical_not(low_first)
        for head in range(KV_DEV):
            first, second = rows_of(head, 0), rows_of(head, 1)
            target[head, 0] = jnp.where(low_first, first, second)
            target[head, 1] = jnp.where(other_first, first, second)

    def weigh(q_part, k_part, masked=False):
        scores = lax.dot_general(
            q_part, k_part, (((1,), (1,)), ((), ())), preferred_element_type=jnp.float32
        )
        expo = jnp.exp(CAP * jnp.tanh(scores * (1.0 / CAP)))
        if masked:
            expo = jnp.where(tile_col <= tile_row, expo, 0.0)
        return expo.astype(jnp.bfloat16), expo[:, :HEAD] + expo[:, HEAD:]

    def blend(weight, v_part):
        return jnp.dot(weight, v_part, preferred_element_type=jnp.float32)

    def attend_own(head):
        def tile(g, carry):
            weight, part = weigh(qrot[head, 2 * g], kpair[head, 0], True)
            num[head, 2 * g] = blend(weight, vpair[head, 0])
            den[head, 2 * g] = part
            weight, part = weigh(qrot[head, 2 * g + 1], kpair[head, 0])
            weight2, part2 = weigh(qrot[head, 2 * g + 1], kpair[head, 1], True)
            num[head, 2 * g + 1] = blend(weight, vpair[head, 0]) + blend(weight2, vpair[head, 1])
            den[head, 2 * g + 1] = part + part2
            return carry

        lax.fori_loop(0, 2, tile, 0)

    def add_parts(total, head, g, to_low, always, either):
        total[head, 2 * g] += jnp.where(to_low, either, 0.0)
        total[head, 2 * g + 1] += always + jnp.where(to_low, 0.0, either)

    def attend(order, head):
        _, _, to_low = meeting(order)

        def tile(g, carry):
            lower, upper = qrot[head, 2 * g], qrot[head, 2 * g + 1]
            weight, part = weigh(upper, kpair[head, 0])
            weight2, part2 = weigh(jnp.where(to_low, lower, upper), kpair[head, 1])
            add_parts(den, head, g, to_low, part, part2)
            always = blend(weight, vpair[head, 0])
            either = blend(weight2, vpair[head, 1])
            add_parts(num, head, g, to_low, always, either)
            return carry

        lax.fori_loop(0, 2, tile, 0)

    def weigh_last(order, head):
        _, _, to_low = meeting(order)

        def tile(g, carry):
            lower, upper = qrot[head, 2 * g], qrot[head, 2 * g + 1]
            weight, part = weigh(upper, kpair[head, 0])
            weight2, part2 = weigh(jnp.where(to_low, lower, upper), kpair[head, 1])
            kept_weight[head, 2 * g] = weight
            kept_weight[head, 2 * g + 1] = weight2
            add_parts(den, head, g, to_low, part, part2)
            return carry

        lax.fori_loop(0, 2, tile, 0)

    def blend_last(order, head):
        _, _, to_low = meeting(order)

        def tile(g, carry):
            always = blend(kept_weight[head, 2 * g], vpair[head, 0])
            either = blend(kept_weight[head, 2 * g + 1], vpair[head, 1])
            add_parts(num, head, g, to_low, always, either)
            return carry

        lax.fori_loop(0, 2, tile, 0)

    def share(to, e, source_at, target_at, count):
        index = len(shares)
        copy = pltpu.make_async_remote_copy(
            src_ref=chosen.at[e + 2 if to else e, pl.ds(source_at, count)],
            dst_ref=arrived.at[e, pl.ds(target_at, count)],
            send_sem=pick_send.at[index],
            recv_sem=pick_recv.at[index],
            device_id=(req, peers[e + 2 if to else e]),
            device_id_type=MESH,
        )
        copy.start()
        sent.append(copy)
        shares.append(copy)

    shares = []

    def own_keys_and_first():
        prepare(0)
        attend_own(0)

    def first_of(order):
        prepare(order)
        attend(order, 0)

    def lens_along_y():
        mate_copy.wait_recv()
        y_copy.start()
        sent.append(y_copy)

    def lens_along_x():
        y_copy.wait_recv()
        for copy in x_copies:
            copy.start()
            sent.append(copy)

    y_copy = len_copy(1, (req // 2) * 2, 2, y_mate)
    x_copies = [len_copy(2 + i, (req // 4) * 4, 4, x_mates[i]) for i in range(3)]

    work = {
        0: [own_keys_and_first],
        1: [lambda: attend_own(1)],
        2: [lens_along_y],
        4: [lens_along_x],
        5: [lambda: first_of(1)],
        6: [lambda: attend(1, 1)],
        7: [lambda: first_of(2)],
        8: [lambda: attend(2, 1)],
        9: [lambda: first_of(3), lambda: attend(3, 1)],
        10: [lambda: first_of(4), lambda: attend(4, 1)],
    }
    got = [0]

    def receive(upto):
        while got[0] <= upto:
            for side in range(2):
                copies[side][got[0]].wait_recv()
            got[0] += 1

    for step in range(12):
        for side in range(2):
            copies[side][step].wait_send()
        following = step + DEPTH
        if following < 14:
            receive(following - 4)
            for side in range(2):
                copies[side][following].start()
        for unit in work.get(step, []):
            receive(4 * ((step - 1) // 4) - 1)
            unit()
    share(0, 1, 0, 0, 5)
    for e in (2, 3):
        share(1, e, 2 - 2 * parity, 1, 2)
        share(0, e, 0, 0, 1)
    receive(11)
    prepare(5)
    attend(5, 0)
    attend(5, 1)
    prepare(6)
    attend(6, 0)
    attend(6, 1)
    for e in (1, 2, 3):
        share(0, e, 5, 5, 1)
        share(0, e, 7, 7, 1)
    for e in (2, 3):
        share(1, e, 4 - 2 * parity, 3, 2)
    receive(12)
    prepare_keys(7)
    weigh_last(7, 0)
    weigh_last(7, 1)
    receive(13)
    prepare_values(7)
    blend_last(7, 0)
    for e in (1, 2, 3):
        share(0, e, 6, 6, 1)
    blend_last(7, 1)

    for copy in x_copies:
        copy.wait_recv()
    length = jnp.zeros((8, 128), jnp.int32)
    for p in range(16):
        length = length + pick(group_of[p] == req, lens[p])
    length = length[0:1, :]

    for half in range(2):
        rows = slice(half * BLOCK, (half + 1) * BLOCK)
        live = row + q_block[half] * BLOCK < jnp.broadcast_to(length, (BLOCK, HEAD))
        lower_here = first_low if half == 0 else jnp.logical_not(first_low)
        for head in range(2 * KV_DEV):
            at = (head % 2) * 2
            parts = jnp.where(lower_here, den[head // 2, at], den[head // 2, at + 1])
            total = jnp.sum(parts, axis=1, keepdims=True)
            value = jnp.where(lower_here, num[head // 2, at], num[head // 2, at + 1]) / total
            out_ref[rows, head * HEAD : (head + 1) * HEAD] = jnp.where(live, value, 0.0).astype(jnp.bfloat16)

    own_residue = jnp.int32(0)
    for r in range(RESIDUES):
        own_residue = own_residue + pick(rank_of[0, r] == me, r)
    p_row = lax.broadcasted_iota(jnp.int32, (HEAD, HEAD), 0)
    p_col = lax.broadcasted_iota(jnp.int32, (HEAD, HEAD), 1)
    place = p_col % 8
    for order in range(8):
        source = (slot + SLOTS - ORDER[order]) % SLOTS
        for half in range(2):
            here = p_col // 8 == 2 * shelf(ORDER[order]) + half
            place = place + pick(here, table[0, half, source] * 8)
    kept = p_row * RESIDUES + own_residue < jnp.broadcast_to(length, (HEAD, HEAD))
    placed = jnp.where(jnp.logical_and(place == p_row, kept), 1.0, 0.0).astype(jnp.bfloat16)

    for copy in shares:
        copy.wait_recv()
    width = KV_DEV * HEAD
    for e in range(4):
        from_head = head_group if e == 0 else quad_peer(e)
        data = chosen[0] if e == 0 else arrived[e]
        data = data.reshape(8 * 16, 2 * width)
        moved = jnp.dot(placed, data, preferred_element_type=jnp.float32).astype(jnp.bfloat16)
        for kind in range(2):
            start = pl.multiple_of(kind * HEAD_DIVISIONS * width + from_head * width, width)
            cache_ref[:, pl.ds(start, width)] = moved[:, kind * width : (kind + 1) * width]

    for step in (12, 13):
        for side in range(2):
            copies[side][step].wait_send()
    for copy in sent:
        copy.wait_send()


def put_out(out_ref, cache_ref, out_to, cache_to, sem):
    first = pltpu.make_async_copy(out_ref, out_to, sem.at[0])
    second = pltpu.make_async_copy(cache_ref, cache_to, sem.at[1])
    first.start()
    second.start()
    first.wait()
    second.wait()


def on_device(queries, keys, values, block_map, lengths, group_of_prompt, decode_rank):
    rows = queries.shape[2]
    wide, narrow = queries.shape[3], keys.shape[3]
    anywhere = pl.BlockSpec(memory_space=pltpu.HBM)
    scalars = pl.BlockSpec(memory_space=pltpu.SMEM)
    vmem = pl.BlockSpec(memory_space=pltpu.VMEM)
    dma = pltpu.SemaphoreType.DMA
    bf16, f32 = jnp.bfloat16, jnp.float32
    out, cache = pl.pallas_call(
        kernel,
        out_shape=(
            jax.ShapeDtypeStruct((rows, wide), bf16),
            jax.ShapeDtypeStruct((rows // HEAD_DIVISIONS, 2048), bf16),
        ),
        in_specs=[anywhere] * 3 + [scalars] * 4,
        out_specs=(vmem, vmem),
        scratch_shapes=[
            pltpu.VMEM((rows, wide), bf16),
            pltpu.VMEM((SLOTS, rows, narrow), bf16),
            pltpu.VMEM((SLOTS, rows, narrow), bf16),
            pltpu.VMEM((KV_DEV, 4, BLOCK, HEAD), bf16),
            pltpu.VMEM((KV_DEV, rows, HEAD), bf16),
            pltpu.VMEM((KV_DEV, 4, BLOCK, HEAD), f32),
            pltpu.VMEM((KV_DEV, 4, BLOCK, HEAD), f32),
            pltpu.VMEM((BLOCK, HEAD), f32),
            pltpu.VMEM((BLOCK, HEAD), f32),
            pltpu.VMEM((2 * SLOTS, HEAD), f32),
            pltpu.VMEM((2 * SLOTS, HEAD), f32),
            pltpu.VMEM((96, 2 * BLOCK), bf16),
            pltpu.VMEM((6, SLOTS, 16, 2 * narrow), bf16),
            pltpu.VMEM((HEAD_DIVISIONS, SLOTS, 16, 2 * narrow), bf16),
            pltpu.VMEM((16, 8, 128), jnp.int32),
            pltpu.VMEM((KV_DEV, 2, BLOCK, HEAD), bf16),
            pltpu.VMEM((KV_DEV, 2, BLOCK, HEAD), bf16),
            pltpu.VMEM((KV_DEV, 4, BLOCK, BLOCK), bf16),
            dma((3,)),
            dma((2, 4, 4)),
            dma((SLOTS, 4)),
            dma((16,)),
            dma((16,)),
            dma((5,)),
            dma((5,)),
        ],
        compiler_params=pltpu.CompilerParams(collective_id=0, has_side_effects=True, vmem_limit_bytes=32 * 2**20),
    )(
        *[pltpu.with_memory_space_constraint(a, pltpu.HBM) for a in (
            queries.reshape(rows, wide), keys.reshape(rows, narrow), values.reshape(rows, narrow),
            jnp.swapaxes(block_map, 1, 2),
        )],
        lengths,
        *[pltpu.with_memory_space_constraint(a, pltpu.HBM) for a in (group_of_prompt, decode_rank)],
    )
    out, cache = pl.pallas_call(
        put_out,
        out_shape=(jax.ShapeDtypeStruct(out.shape, bf16), jax.ShapeDtypeStruct(cache.shape, bf16)),
        in_specs=[pl.BlockSpec(memory_space=pltpu.VMEM)] * 2,
        compiler_params=pltpu.CompilerParams(vmem_limit_bytes=8 * 2**20),
        out_specs=(pl.BlockSpec(memory_space=pl.ANY),) * 2,
        scratch_shapes=[dma((2,))],
    )(out, cache)
    return out[None, None], cache[None]


def solution(mesh):
    placed = (
        P("req", "blk", None, None),
        P("req", "blk", None, None),
        P("req", "blk", None, None),
        P("req", None, None),
        P("req"),
        P(),
        P("req", None),
    )
    return jax.shard_map(
        on_device,
        mesh=mesh,
        in_specs=placed,
        out_specs=(P("req", "blk", None, None), P("req", "blk", None)),
        check_vma=False,
    )
```
